256 devices in a mesh: wide: 16 (over z_hi, x), narrow: 16 (over z_lo, y, core).
Axes of the slice: x: 4, y: 4, z: 8 (z_hi: 4, z_lo: 2; z = z_hi * 2 + z_lo), core: 2. Of those that a mesh axis runs over, the one named last changes fastest.
Arguments:
- node: bfloat16 [256, 256, 256], P('narrow'), may hold values from -6 to 6
- right_side: bfloat16 [256, 256, 256], P('narrow'), may hold values from -16 to 16
- leg_ops: bfloat16 [3, 12, 256, 256], replicated, may hold values from -0.375 to 0.375
- op_index: int32 [64, 3], P('wide'), may hold values from 0 to 11, as said below
- offsets: int32 [64], P('wide'), may hold values from 0 to 7
Outputs:
- new_node: float32 [256, 256, 256], P('narrow')
The draws below stay inside these ranges and needn't reach their ends.
Inputs may be any that keep to these rules, and one draw needn't show every extreme that they name: `op_index`: no two triples name the same pair of leg b and leg c operators; every operator of each leg is named by some triple.
All inputs are finite; a program needn't handle non-finite values.
Results may differ from the reference program's by a relative error of at most 0.0019.
Values may be sent and summed in bfloat16 or wider, within the bound.
No kernel may reach another device: no remote copies, remote signals or barrier semaphores. Data moves between devices by JAX's collectives and lax.ppermute only.
A program may use at most 64 MiB of HBM per device.

```python
import math
import jax
import jax.numpy as jnp

BOND = 256
KOPS = 12
SECTORS = 8
TRIPLES = 64


def draw_op_index(key, part):
    subkeys = jax.random.split(jax.random.fold_in(key, 7321), 5)
    position = jnp.arange(TRIPLES, dtype=jnp.int32)
    perm_a = jax.random.permutation(subkeys[0], KOPS).astype(jnp.int32)
    perm_b = jax.random.permutation(subkeys[1], KOPS).astype(jnp.int32)
    perm_c = jax.random.permutation(subkeys[2], KOPS).astype(jnp.int32)
    slot_row = position % KOPS
    slot_col = (position // KOPS + position % KOPS) % KOPS
    filler = jax.random.randint(subkeys[3], (TRIPLES,), 0, KOPS).astype(jnp.int32)
    leg_a = jnp.where(position < KOPS, perm_a[slot_row], filler)
    lookup_table = jnp.stack([leg_a, perm_b[slot_row], perm_c[slot_col]], axis=1)
    shuffle = jax.random.permutation(subkeys[4], TRIPLES).astype(jnp.int32)
    return lookup_table[shuffle].astype(jnp.int32)


def place_ends(entries, own_key, smallest, top_value):
    shape = entries.shape
    index_at = [jax.random.randint(jax.random.fold_in(own_key, axis), (), 0, shape[axis]) for axis in range(len(shape))]
    entries = entries.at[tuple(index_at)].set(smallest)
    longest = shape.index(max(shape))
    index_at[longest] = (index_at[longest] + 1) % shape[longest]
    return entries.at[tuple(index_at)].set(top_value)


def level_of(rng, dims, shards, low, high):
    loudness, own = 1.0, jax.random.fold_in(rng, 6)
    for dim, parts in shards:
        heights = jnp.exp(jax.random.uniform(jax.random.fold_in(own, dim), (parts,), jnp.float32, low / len(shards), high / len(shards)))
        loudness = loudness * jnp.repeat(heights, dims[dim] // parts).reshape([-1 if axis == dim else 1 for axis in range(len(dims))])
    return loudness


def centred(rng, extent, width, most, cuts=(), held_as=jnp.bfloat16):
    result = jax.random.normal(rng, extent, jnp.float32) * width
    if len(cuts) > 0:
        result = level_of(rng, extent, cuts, -0.22, 0.18) * result
    return jnp.clip(result, min=-most, max=most).astype(held_as)


def setup_inputs(seed: int = 0) -> dict:
    arg_keys = jax.random.split(jax.random.key(seed), 6)
    return {
        "node": centred(arg_keys[0], (BOND, BOND, BOND), 1.0, 6.0, ((0, 16),)),
        "right_side": centred(arg_keys[1], (BOND, BOND, BOND), 4.0, 16.0, ((0, 16),)),
        "leg_ops": centred(arg_keys[2], (3, KOPS, BOND, BOND), BOND ** -0.5, 0.375),
        "op_index": draw_op_index(jax.random.fold_in(arg_keys[5], 71), 0),
        "offsets": place_ends(jax.random.randint(arg_keys[4], (TRIPLES,), 0, SECTORS), jax.random.fold_in(arg_keys[4], 1), 0, SECTORS - 1).astype(jnp.int32),
    }


def reference(node, right_side, leg_ops, op_index, offsets):
    whole = node.astype(jnp.float32)
    sector = BOND // SECTORS
    sigma = jnp.zeros((BOND, BOND, BOND), jnp.float32)
    for triple in range(TRIPLES):
        op_a = leg_ops[0, op_index[triple, 0]].astype(jnp.float32)
        op_b = leg_ops[1, op_index[triple, 1]].astype(jnp.float32)
        op_c = leg_ops[2, op_index[triple, 2]].astype(jnp.float32)
        first = jnp.einsum('abc,qc->abq', whole, op_c).astype(jnp.bfloat16).astype(jnp.float32)
        second = jnp.einsum('pb,abq->apq', op_b, first).astype(jnp.bfloat16).astype(jnp.float32)
        shifted = jnp.roll(op_a, offsets[triple] * sector, axis=0)
        sigma = sigma + jnp.einsum('ra,apq->rpq', shifted, second)
    tau = 0.5 / math.sqrt(TRIPLES)
    return whole + tau * (right_side.astype(jnp.float32) - sigma)
```

```python
import functools
import math

import jax
import jax.numpy as jnp
from jax import lax
from jax.experimental import pallas as pl
from jax.experimental.pallas import tpu as pltpu
from jax.sharding import PartitionSpec as P

SECTORS = 8
Z_HI, X_SIZE, Z_LO, Y_SIZE, CORES = 4, 4, 2, 4, 2
NT = (((1,), (1,)), ((), ()))
NN = (((1,), (0,)), ((), ()))
PARAMS = pltpu.CompilerParams(vmem_limit_bytes=60 * 1024 * 1024)


def pairs_of(move):
    out = []
    for z_hi in range(Z_HI):
        for x in range(X_SIZE):
            for z_lo in range(Z_LO):
                for y in range(Y_SIZE):
                    for core in range(CORES):
                        a, b, c, d, e = move(z_hi, x, z_lo, y, core)
                        there = (a % Z_HI) * X_SIZE + b % X_SIZE
                        block = ((c % Z_LO) * Y_SIZE + d % Y_SIZE) * CORES + e % CORES
                        here = (z_hi * X_SIZE + x) * 16 + (z_lo * Y_SIZE + y) * CORES + core
                        out.append((here, there * 16 + block))
    return out


def send(value, dz_hi=0, dx=0, dz_lo=0, dy=0, dcore=0):
    def move(z_hi, x, z_lo, y, core):
        return z_hi + dz_hi, x + dx, z_lo + dz_lo, y + dy, core + dcore

    return lax.ppermute(value, ("wide", "narrow"), pairs_of(move))


def swap_wide(value, bit):
    pairs = [(w, w ^ bit) for w in range(16)]
    return lax.ppermute(value, "wide", pairs)


def first_kernel(node_ref, ops_ref, out_ref, scratch):
    rows = ops_ref.shape[0]
    for a in range(16):
        block = lax.dot_general(ops_ref[...], node_ref[a], NT, preferred_element_type=jnp.float32)
        for c in range(2):
            scratch[c, pl.ds(a, rows, stride=16), :] = block[:, c * 128 : (c + 1) * 128]
    for c in range(2):
        out_ref[:, c * 128 : (c + 1) * 128] = scratch[c].astype(jnp.bfloat16)


def first_of(node, ops):
    rows = ops.shape[0] * 16
    return pl.pallas_call(
        first_kernel,
        out_shape=jax.ShapeDtypeStruct((rows, 256), jnp.bfloat16),
        scratch_shapes=[pltpu.VMEM((2, rows, 128), jnp.float32)],
        compiler_params=PARAMS,
        cost_estimate=pl.CostEstimate(flops=2 * rows * 65536, bytes_accessed=3 << 20, transcendentals=0),
        name="first_leg",
    )(node, ops)


def columns_kernel(place, ops_ref, out_ref):
    base, core = place[0], place[1]
    lane = lax.broadcasted_iota(jnp.int32, (256, 128), 1) % 32
    source = base + jnp.where(lane < 16, core * 16 + lane, (1 - core) * 16 + lane - 16)
    row = lax.broadcasted_iota(jnp.int32, (256, 128), 0)
    pick = jnp.where(row == source, 1.0, 0.0).astype(jnp.bfloat16)
    for i in range(12):
        block = lax.dot_general(ops_ref[0, i], pick, NN, preferred_element_type=jnp.float32)
        block = block.astype(jnp.bfloat16)
        out_ref[i, :256] = block
        out_ref[i, 256:] = block


def columns_of(place, leg_ops):
    return pl.pallas_call(
        columns_kernel,
        out_shape=jax.ShapeDtypeStruct((12, 512, 128), jnp.bfloat16),
        grid_spec=pltpu.PrefetchScalarGridSpec(
            num_scalar_prefetch=1,
            grid=(1,),
            in_specs=[pl.BlockSpec((1, 12, 256, 256), lambda g, s: (0, 0, 0, 0))],
            out_specs=pl.BlockSpec((12, 512, 128), lambda g, s: (0, 0, 0)),
        ),
        compiler_params=PARAMS,
        cost_estimate=pl.CostEstimate(flops=2 * 3072 * 256 * 128, bytes_accessed=3 << 20, transcendentals=0),
        name="leg_a_columns",
    )(place, leg_ops)


def main_kernel(table, blocks, own_ref, sib_ref, ops_ref, cols_ref, keep_ref, m1_ref, m2_ref, m3_ref, second, a_abs, a_rel):
    lane = lax.broadcasted_iota(jnp.int32, (16, 128), 1) // 32

    def fill(g, carry):
        starts = []
        for s in range(4):
            t = g * 4 + s
            starts.append((table[t, 0], pl.multiple_of(256 - 32 * table[t, 3], 32)))
        for blk in range(16):
            value = None
            for s, (i, start) in enumerate(starts):
                part = cols_ref[i, pl.ds(start + 16 * blk, 16), :]
                value = part if value is None else jnp.where(lane == s, part, value)
            a_abs[g, pl.ds(16 * blk, 16), :] = value
        return carry

    lax.fori_loop(0, 16, fill, 0)
    for blk in range(16):
        source = pl.multiple_of(blocks[blk] * 16, 16)
        for g in range(16):
            a_rel[pl.ds(16 * blk, 16), g * 128 : (g + 1) * 128] = a_abs[g, pl.ds(source, 16), :]

    def step(t, carry):
        j, k = table[t, 1], table[t, 2]
        op = ops_ref[0, j]
        for half, ref in enumerate((own_ref, sib_ref)):
            value = lax.dot_general(ref[k], op, NT, preferred_element_type=jnp.float32)
            value = value.astype(jnp.bfloat16)
            for q in range(8):
                where = pl.multiple_of(t * 32 + half * 16, 16)
                second[q, pl.ds(where, 16), :] = value[q * 16 : q * 16 + 16]
        return carry

    lax.fori_loop(0, 64, step, 0, unroll=4)
    for q in range(8):
        value = lax.dot_general(a_rel[...], second[q], NN, preferred_element_type=jnp.float32)
        keep_ref[q] = value[:64]
        m1_ref[q] = value[64:128].astype(jnp.bfloat16)
        m2_ref[q] = value[128:192].astype(jnp.bfloat16)
        m3_ref[q] = value[192:].astype(jnp.bfloat16)


def main_of(table, blocks, own, sib, leg_ops, cols):
    whole3 = lambda g, s, u: (0, 0, 0)
    return pl.pallas_call(
        main_kernel,
        out_shape=[jax.ShapeDtypeStruct((8, 64, 256), jnp.float32)]
        + [jax.ShapeDtypeStruct((8, 64, 256), jnp.bfloat16)] * 3,
        grid_spec=pltpu.PrefetchScalarGridSpec(
            num_scalar_prefetch=2,
            grid=(1,),
            in_specs=[
                pl.BlockSpec((12, 128, 256), whole3),
                pl.BlockSpec((12, 128, 256), whole3),
                pl.BlockSpec((1, 12, 256, 256), lambda g, s, u: (1, 0, 0, 0)),
                pl.BlockSpec((12, 512, 128), whole3),
            ],
            out_specs=[pl.BlockSpec((8, 64, 256), whole3)] * 4,
            scratch_shapes=[
                pltpu.VMEM((8, 2048, 256), jnp.bfloat16),
                pltpu.VMEM((16, 256, 128), jnp.bfloat16),
                pltpu.VMEM((256, 2048), jnp.bfloat16),
            ],
        ),
        compiler_params=PARAMS,
        cost_estimate=pl.CostEstimate(flops=128 * 2 * 256**3, bytes_accessed=8 << 20, transcendentals=0),
        name="two_legs",
    )(table, blocks, own, sib, leg_ops, cols)


def y_kernel(keep_ref, r1_ref, r2_ref, r3_ref, keep_out, m01_ref, m10_ref, m11_ref):
    f32 = jnp.float32
    for q in range(8):
        value = keep_ref[q] + r1_ref[q].astype(f32) + r2_ref[q].astype(f32) + r3_ref[q].astype(f32)
        keep_out[q] = value[:16]
        m01_ref[q] = value[16:32].astype(jnp.bfloat16)
        m10_ref[q] = value[32:48].astype(jnp.bfloat16)
        m11_ref[q] = value[48:].astype(jnp.bfloat16)


def y_sum(keep, r1, r2, r3):
    return pl.pallas_call(
        y_kernel,
        out_shape=[jax.ShapeDtypeStruct((8, 16, 256), jnp.float32)]
        + [jax.ShapeDtypeStruct((8, 16, 256), jnp.bfloat16)] * 3,
        compiler_params=PARAMS,
        name="sum_y",
    )(keep, r1, r2, r3)


def z_kernel(core_ref, keep_ref, r01_ref, r10_ref, r11_ref, out_ref, scratch):
    f32 = jnp.float32
    core = core_ref[0]
    for q in range(8):
        mine = keep_ref[q] + r10_ref[q].astype(f32)
        other = r01_ref[q].astype(f32) + r11_ref[q].astype(f32)
        low = jnp.where(core == 0, mine, other)
        high = jnp.where(core == 0, other, mine)
        for c in range(2):
            scratch[c, pl.ds(q, 16, stride=16), :] = low[:, c * 128 : (c + 1) * 128]
            scratch[c, pl.ds(8 + q, 16, stride=16), :] = high[:, c * 128 : (c + 1) * 128]
    for c in range(2):
        out_ref[:, c * 128 : (c + 1) * 128] = scratch[c].astype(jnp.bfloat16)


def z_sum(core, keep, r01, r10, r11):
    vmem = pl.BlockSpec(memory_space=pltpu.VMEM)
    return pl.pallas_call(
        z_kernel,
        out_shape=jax.ShapeDtypeStruct((256, 256), jnp.bfloat16),
        in_specs=[pl.BlockSpec(memory_space=pltpu.SMEM)] + [vmem] * 4,
        out_specs=vmem,
        scratch_shapes=[pltpu.VMEM((2, 256, 128), jnp.float32)],
        compiler_params=PARAMS,
        name="sum_z",
    )(core, keep, r01, r10, r11)


def last_kernel(tau, place, own_ref, left_ref, right_ref, fl_ref, fr_ref, node_ref, side_ref, out_ref, sigma):
    f32 = jnp.float32
    z_hi, x = place[0], place[1]

    def put(ref, slot, dz, dx):
        w = lax.rem(z_hi - dz + 4, 4) * 4 + lax.rem(x - dx + 4, 4)
        sigma[pl.ds(pl.multiple_of(w * 16, 16), 16), :] = ref[slot]

    for dz in range(4):
        put(own_ref, dz, dz, 0)
        put(left_ref, dz, dz, 1)
        put(right_ref, dz, dz, 3)
        if dz < 2:
            put(fl_ref, dz, dz, 2)
        else:
            put(fr_ref, dz - 2, dz, 2)
    row = lax.broadcasted_iota(jnp.int32, (256, 256), 0)
    column = lax.broadcasted_iota(jnp.int32, (256, 256), 1)
    eye = jnp.where(row == column, 1.0, 0.0).astype(jnp.bfloat16)
    turned = lax.dot_general(eye, sigma[...], NT, preferred_element_type=f32)
    out_ref[0] = node_ref[0].astype(f32) + tau * (side_ref[0].astype(f32) - turned)


def last_of(tau, place, own, left, right, fl, fr, node, side):
    def piece(n):
        return pl.BlockSpec((n, 16, 256), lambda r, s: (0, r, 0))

    row = pl.BlockSpec((1, 256, 256), lambda r, s: (r, 0, 0))
    return pl.pallas_call(
        functools.partial(last_kernel, tau),
        out_shape=jax.ShapeDtypeStruct((16, 256, 256), jnp.float32),
        grid_spec=pltpu.PrefetchScalarGridSpec(
            num_scalar_prefetch=1,
            grid=(16,),
            in_specs=[piece(4), piece(4), piece(4), piece(2), piece(2), row, row],
            out_specs=row,
            scratch_shapes=[pltpu.VMEM((256, 256), jnp.bfloat16)],
        ),
        compiler_params=PARAMS,
        name="update",
    )(place, own, left, right, fl, fr, node, side)


def per_device(node, right_side, leg_ops, op_index, offsets):
    wide, narrow = lax.axis_index("wide"), lax.axis_index("narrow")
    z_hi, x = wide // 4, wide % 4
    z_lo, y, core = narrow // 8, (narrow // 2) % 4, narrow % 2
    tau = 0.5 / math.sqrt(op_index.shape[0] * lax.axis_size("wide"))

    with jax.named_scope("node_swap"):
        sibling = send(node, dcore=1)
    with jax.named_scope("index"):
        mine = jnp.concatenate([op_index, offsets[:, None]], axis=1).reshape(1, 16)
        table = jnp.where(lax.broadcasted_iota(jnp.int32, (16, 16), 0) == wide, mine, 0)
        for bit in (1, 2, 4, 8):
            table = table + swap_wide(table, bit)
        table = table.reshape(64, 4)

    with jax.named_scope("ops_c"):
        ops_c = lax.dynamic_slice(leg_ops, (2, 0, wide * 16 + core * 8, 0), (1, 12, 8, 256))
        ops_c = ops_c.reshape(96, 256)
    own = first_of(node, ops_c).reshape(12, 128, 256)
    cols = columns_of(jnp.stack([(narrow // 2) * 32, core]), leg_ops)
    sib = first_of(sibling, ops_c).reshape(12, 128, 256)

    order = []
    for dy in range(4):
        for dz in range(2):
            for dc in range(2):
                order.append(((z_lo + dz) % 2) * 8 + ((y + dy) % 4) * 2 + (core + dc) % 2)
    keep, m1, m2, m3 = main_of(table, jnp.stack(order), own, sib, leg_ops, cols)
    with jax.named_scope("y_stage"):
        r1, r3, r2 = send(m1, dy=1), send(m3, dy=3), send(m2, dy=2)
    keep, m01, m10, m11 = y_sum(keep, r1, r2, r3)
    with jax.named_scope("z_stage"):
        r10, r11, r01 = send(m10, dz_lo=1), send(m11, dz_lo=1, dcore=1), send(m01, dcore=1)
    piece = z_sum(jnp.stack([core]), keep, r01, r10, r11)
    with jax.named_scope("gather_z"):
        got = [piece] + [send(piece, dz_hi=d) for d in (1, 2, 3)]
        got = jnp.stack(got)
    with jax.named_scope("gather_x"):
        left, right = send(got, dx=1), send(got, dx=3)
        fl, fr = send(left[:2], dx=1), send(right[2:], dx=3)
    place = jnp.stack([z_hi, x])
    return last_of(tau, place, got, left, right, fl, fr, node, right_side)


def solution(mesh):
    in_specs = (P("narrow", None, None), P("narrow", None, None), P(), P("wide", None), P("wide"))
    out_specs = P("narrow", None, None)
    return jax.shard_map(
        per_device, mesh=mesh, in_specs=in_specs, out_specs=out_specs, check_vma=False
    )
```

```python
import functools
import math

import jax
import jax.numpy as jnp
from jax import lax
from jax.experimental import pallas as pl
from jax.experimental.pallas import tpu as pltpu
from jax.sharding import PartitionSpec as P

Z_HI, X_SIZE, Z_LO, Y_SIZE, CORES = 4, 4, 2, 4, 2
NT = (((1,), (1,)), ((), ()))
NN = (((1,), (0,)), ((), ()))


def grant(mib):
    return pltpu.CompilerParams(vmem_limit_bytes=mib << 20)


def pairs_of(move):
    out = []
    for z_hi in range(Z_HI):
        for x in range(X_SIZE):
            for z_lo in range(Z_LO):
                for y in range(Y_SIZE):
                    for core in range(CORES):
                        a, b, c, d, e = move(z_hi, x, z_lo, y, core)
                        there = (a % Z_HI) * X_SIZE + b % X_SIZE
                        block = ((c % Z_LO) * Y_SIZE + d % Y_SIZE) * CORES + e % CORES
                        here = (z_hi * X_SIZE + x) * 16 + (z_lo * Y_SIZE + y) * CORES + core
                        out.append((here, there * 16 + block))
    return out


def send(value, dz_hi=0, dx=0, dz_lo=0, dy=0, dcore=0):
    def move(z_hi, x, z_lo, y, core):
        return z_hi + dz_hi, x + dx, z_lo + dz_lo, y + dy, core + dcore

    return lax.ppermute(value, ("wide", "narrow"), pairs_of(move))


def swap_wide(value, bit):
    pairs = [(w, w ^ bit) for w in range(16)]
    return lax.ppermute(value, "wide", pairs)


def leg_c(node_ref, ops, scratch):
    rows = ops.shape[0]
    for a in range(16):
        block = lax.dot_general(ops, node_ref[a], NT, preferred_element_type=jnp.float32)
        for c in range(2):
            scratch[c, pl.ds(a, rows, stride=16), :] = block[:, c * 128 : (c + 1) * 128]


def put_first(scratch, out_ref):
    for k in range(12):
        for c in range(2):
            value = scratch[c, k * 128 : (k + 1) * 128].astype(jnp.bfloat16)
            out_ref[k, 0, :, c * 128 : (c + 1) * 128] = value


def prep_kernel(node_ref, leg_a_ref, legs_ref, first_ref, cols_ref, ops_ref, tiles, wide_tiles, scratch, sem):
    wide, narrow = lax.axis_index("wide"), lax.axis_index("narrow")
    core = lax.rem(narrow, 2)
    fetch = pltpu.make_async_copy(legs_ref.at[2, :, pl.ds(pl.multiple_of(wide * 16, 16), 16), :], tiles, sem)
    fetch.start()
    lane = lax.broadcasted_iota(jnp.int32, (256, 128), 1) % 32
    source = (narrow - core) * 16 + jnp.where(lane < 16, core * 16 + lane, (1 - core) * 16 + lane - 16)
    row = lax.broadcasted_iota(jnp.int32, (256, 128), 0)
    pick = jnp.where(row == source, 1.0, 0.0).astype(jnp.bfloat16)
    for i in range(12):
        block = lax.dot_general(leg_a_ref[0, i], pick, NN, preferred_element_type=jnp.float32)
        block = block.astype(jnp.bfloat16)
        cols_ref[i, :256] = block
        cols_ref[i, 256:] = block
    fetch.wait()
    wide_tiles[...] = tiles[...].astype(jnp.float32)
    half = [wide_tiles[k, pl.ds(pl.multiple_of(core * 8, 8), 8), :] for k in range(12)]
    ops = jnp.concatenate(half, axis=0).astype(jnp.bfloat16)
    ops_ref[...] = ops
    leg_c(node_ref, ops, scratch)
    put_first(scratch, first_ref)


def prep(node, leg_ops):
    return pl.pallas_call(
        prep_kernel,
        out_shape=[
            jax.ShapeDtypeStruct((12, 2, 128, 256), jnp.bfloat16),
            jax.ShapeDtypeStruct((12, 512, 128), jnp.bfloat16),
            jax.ShapeDtypeStruct((96, 256), jnp.bfloat16),
        ],
        grid=(1,),
        in_specs=[
            pl.BlockSpec((16, 256, 256), lambda g: (0, 0, 0)),
            pl.BlockSpec((1, 12, 256, 256), lambda g: (0, 0, 0, 0)),
            pl.BlockSpec(memory_space=pl.ANY),
        ],
        out_specs=[
            pl.BlockSpec((12, 1, 128, 256), lambda g: (0, 0, 0, 0)),
            pl.BlockSpec((12, 512, 128), lambda g: (0, 0, 0)),
            pl.BlockSpec((96, 256), lambda g: (0, 0)),
        ],
        scratch_shapes=[
            pltpu.VMEM((12, 16, 256), jnp.bfloat16),
            pltpu.VMEM((12, 16, 256), jnp.float32),
            pltpu.VMEM((2, 1536, 128), jnp.float32),
            pltpu.SemaphoreType.DMA(()),
        ],
        compiler_params=grant(17),
        cost_estimate=pl.CostEstimate(flops=2 * 3072 * 256 * 300, bytes_accessed=6 << 20, transcendentals=0),
        name="prep",
    )(node, leg_ops, leg_ops)


def sibling_kernel(node_ref, ops_ref, first_ref, out_ref, scratch):
    del first_ref
    leg_c(node_ref, ops_ref[...], scratch)
    put_first(scratch, out_ref)


def add_sibling(node, ops, first):
    return pl.pallas_call(
        sibling_kernel,
        out_shape=jax.ShapeDtypeStruct((12, 2, 128, 256), jnp.bfloat16),
        grid=(1,),
        in_specs=[
            pl.BlockSpec((16, 256, 256), lambda g: (0, 0, 0)),
            pl.BlockSpec((96, 256), lambda g: (0, 0)),
            pl.BlockSpec(memory_space=pl.ANY),
        ],
        out_specs=pl.BlockSpec((12, 1, 128, 256), lambda g: (0, 1, 0, 0)),
        scratch_shapes=[pltpu.VMEM((2, 1536, 128), jnp.float32)],
        input_output_aliases={2: 0},
        compiler_params=grant(10),
        cost_estimate=pl.CostEstimate(flops=2 * 1536 * 65536, bytes_accessed=3 << 20, transcendentals=0),
        name="sibling",
    )(node, ops, first)


def table_kernel(index_ref, offset_ref, out_ref):
    shape = (16, 128)
    row, lane = lax.broadcasted_iota(jnp.int32, shape, 0), lax.broadcasted_iota(jnp.int32, shape, 1)
    value = jnp.zeros(shape, jnp.int32)
    for t in range(4):
        for m in range(4):
            entry = offset_ref[t] if m == 3 else index_ref[t, m]
            value = jnp.where(lane == t * 4 + m, entry, value)
    out_ref[...] = jnp.where(row == lax.axis_index("wide"), value, 0)


def own_rows(op_index, offsets):
    smem = pl.BlockSpec(memory_space=pltpu.SMEM)
    return pl.pallas_call(
        table_kernel,
        out_shape=jax.ShapeDtypeStruct((16, 128), jnp.int32),
        in_specs=[smem, smem],
        compiler_params=grant(1),
        name="own_rows",
    )(op_index, offsets)


def main_kernel(table, first_ref, ops_ref, cols_ref, keep_ref, m1_ref, m2_ref, m3_ref, second, a_abs, a_rel):
    narrow = lax.axis_index("narrow")
    lane = lax.broadcasted_iota(jnp.int32, (16, 128), 1) // 32

    def fill(g, carry):
        starts = []
        for s in range(4):
            start = pl.multiple_of(256 - 32 * table[g, s * 4 + 3], 32)
            starts.append((table[g, s * 4], start))
        for blk in range(16):
            value = None
            for s, (i, start) in enumerate(starts):
                part = cols_ref[i, pl.ds(start + 16 * blk, 16), :]
                value = part if value is None else jnp.where(lane == s, part, value)
            a_abs[g, pl.ds(16 * blk, 16), :] = value
        return carry

    lax.fori_loop(0, 16, fill, 0)
    core, z_lo = lax.rem(narrow, 2), narrow // 8
    y = lax.rem(narrow // 2, 4)
    for blk in range(16):
        dy, dz, dc = blk // 4, (blk // 2) % 2, blk % 2
        block = lax.rem(z_lo + dz, 2) * 8 + lax.rem(y + dy, 4) * 2 + lax.rem(core + dc, 2)
        source = pl.multiple_of(block * 16, 16)
        for g in range(16):
            a_rel[16 * blk : 16 * blk + 16, g * 128 : (g + 1) * 128] = a_abs[g, pl.ds(source, 16), :]

    def step(g, carry):
        for s in range(4):
            j, k = table[g, s * 4 + 1], table[g, s * 4 + 2]
            lhs = first_ref[k].reshape(256, 256)
            value = lax.dot_general(lhs, ops_ref[0, j], NT, preferred_element_type=jnp.float32)
            value = value.astype(jnp.bfloat16)
            for half in range(2):
                for q in range(8):
                    where = pl.multiple_of(g * 128 + s * 32 + half * 16, 16)
                    source = half * 128 + q * 16
                    second[q, pl.ds(where, 16), :] = value[source : source + 16]
        return carry

    lax.fori_loop(0, 16, step, 0)
    for q in range(8):
        value = lax.dot_general(a_rel[...], second[q], NN, preferred_element_type=jnp.float32)
        keep_ref[q] = value[:64]
        m1_ref[q] = value[64:128].astype(jnp.bfloat16)
        m2_ref[q] = value[128:192].astype(jnp.bfloat16)
        m3_ref[q] = value[192:].astype(jnp.bfloat16)


def main_of(table, first, leg_ops, cols):
    whole3 = lambda g, s: (0, 0, 0)
    return pl.pallas_call(
        main_kernel,
        out_shape=[jax.ShapeDtypeStruct((8, 64, 256), jnp.float32)]
        + [jax.ShapeDtypeStruct((8, 64, 256), jnp.bfloat16)] * 3,
        grid_spec=pltpu.PrefetchScalarGridSpec(
            num_scalar_prefetch=1,
            grid=(1,),
            in_specs=[
                pl.BlockSpec((12, 2, 128, 256), lambda g, s: (0, 0, 0, 0)),
                pl.BlockSpec((1, 12, 256, 256), lambda g, s: (1, 0, 0, 0)),
                pl.BlockSpec((12, 512, 128), whole3),
            ],
            out_specs=[pl.BlockSpec((8, 64, 256), whole3)] * 4,
            scratch_shapes=[
                pltpu.VMEM((8, 2048, 256), jnp.bfloat16),
                pltpu.VMEM((16, 256, 128), jnp.bfloat16),
                pltpu.VMEM((256, 2048), jnp.bfloat16),
            ],
        ),
        compiler_params=grant(28),
        cost_estimate=pl.CostEstimate(flops=128 * 2 * 256**3, bytes_accessed=8 << 20, transcendentals=0),
        name="two_legs",
    )(table, first, leg_ops, cols)


def y_kernel(keep_ref, r1_ref, r2_ref, r3_ref, keep_out, m01_ref, m10_ref, m11_ref):
    f32 = jnp.float32
    for q in range(8):
        value = keep_ref[q] + r1_ref[q].astype(f32) + r2_ref[q].astype(f32) + r3_ref[q].astype(f32)
        keep_out[q] = value[:16]
        m01_ref[q] = value[16:32].astype(jnp.bfloat16)
        m10_ref[q] = value[32:48].astype(jnp.bfloat16)
        m11_ref[q] = value[48:].astype(jnp.bfloat16)


def y_sum(keep, r1, r2, r3):
    return pl.pallas_call(
        y_kernel,
        out_shape=[jax.ShapeDtypeStruct((8, 16, 256), jnp.float32)]
        + [jax.ShapeDtypeStruct((8, 16, 256), jnp.bfloat16)] * 3,
        compiler_params=grant(6),
        name="sum_y",
    )(keep, r1, r2, r3)


def z_kernel(keep_ref, r01_ref, r10_ref, r11_ref, out_ref, scratch):
    f32 = jnp.float32
    core = lax.rem(lax.axis_index("narrow"), 2)
    for q in range(8):
        mine = keep_ref[q] + r10_ref[q].astype(f32)
        other = r01_ref[q].astype(f32) + r11_ref[q].astype(f32)
        low = jnp.where(core == 0, mine, other)
        high = jnp.where(core == 0, other, mine)
        for c in range(2):
            scratch[c, pl.ds(q, 16, stride=16), :] = low[:, c * 128 : (c + 1) * 128]
            scratch[c, pl.ds(8 + q, 16, stride=16), :] = high[:, c * 128 : (c + 1) * 128]
    for c in range(2):
        out_ref[:, c * 128 : (c + 1) * 128] = scratch[c].astype(jnp.bfloat16)


def z_sum(keep, r01, r10, r11):
    vmem = pl.BlockSpec(memory_space=pltpu.VMEM)
    return pl.pallas_call(
        z_kernel,
        out_shape=jax.ShapeDtypeStruct((256, 256), jnp.bfloat16),
        in_specs=[vmem] * 4,
        out_specs=vmem,
        scratch_shapes=[pltpu.VMEM((2, 256, 128), jnp.float32)],
        compiler_params=grant(3),
        name="sum_z",
    )(keep, r01, r10, r11)


def last_kernel(tau, own_ref, left_ref, right_ref, fl_ref, fr_ref, node_ref, side_ref, out_ref, sigma):
    f32 = jnp.float32
    wide = lax.axis_index("wide")
    z_hi, x = wide // 4, lax.rem(wide, 4)
    row = lax.broadcasted_iota(jnp.int32, (256, 256), 0)
    column = lax.broadcasted_iota(jnp.int32, (256, 256), 1)
    eye = jnp.where(row == column, 1.0, 0.0).astype(jnp.bfloat16)
    for r in range(ROWS):
        for dz in range(4):
            two = fl_ref[dz] if dz < 2 else fr_ref[dz - 2]
            for dx, value in ((0, own_ref[dz]), (1, left_ref[dz]), (3, right_ref[dz]), (2, two)):
                w = lax.rem(z_hi - dz + 4, 4) * 4 + lax.rem(x - dx + 4, 4)
                place = pl.ds(pl.multiple_of(w * 16, 16), 16)
                sigma[r, place, :] = value[r * 16 : (r + 1) * 16]
    for r in range(ROWS):
        turned = lax.dot_general(eye, sigma[r], NT, preferred_element_type=f32)
        out_ref[r] = node_ref[r].astype(f32) + tau * (side_ref[r].astype(f32) - turned)


ROWS = 4


def last_of(tau, own, left, right, fl, fr, node, side):
    def piece(n):
        return pl.BlockSpec((n, ROWS * 16, 256), lambda r: (0, r, 0))

    row = pl.BlockSpec((ROWS, 256, 256), lambda r: (r, 0, 0))
    return pl.pallas_call(
        functools.partial(last_kernel, tau),
        out_shape=jax.ShapeDtypeStruct((16, 256, 256), jnp.float32),
        grid=(16 // ROWS,),
        in_specs=[piece(4), piece(4), piece(4), piece(2), piece(2), row, row],
        out_specs=row,
        scratch_shapes=[pltpu.VMEM((ROWS, 256, 256), jnp.bfloat16)],
        compiler_params=grant(16),
        name="update",
    )(own, left, right, fl, fr, node, side)


def per_device(node, right_side, leg_ops, op_index, offsets):
    tau = 0.5 / math.sqrt(op_index.shape[0] * lax.axis_size("wide"))
    table = own_rows(op_index, offsets)
    for step in range(4):
        table = table + swap_wide(table, 1 << step)
    sibling = send(node, dcore=1)
    first, cols, ops_c = prep(node, leg_ops)
    first = add_sibling(sibling, ops_c, first)
    keep, m1, m2, m3 = main_of(table, first, leg_ops, cols)
    r1, r3, r2 = send(m1, dy=1), send(m3, dy=3), send(m2, dy=2)
    keep, m01, m10, m11 = y_sum(keep, r1, r2, r3)
    r10, r11, r01 = send(m10, dz_lo=1), send(m11, dz_lo=1, dcore=1), send(m01, dcore=1)
    piece = z_sum(keep, r01, r10, r11)
    got = [piece] + [send(piece, dz_hi=d) for d in (1, 2, 3)]
    got = jnp.stack(got)
    left, right = send(got, dx=1), send(got, dx=3)
    fl, fr = send(left[:2], dx=1), send(right[2:], dx=3)
    return last_of(tau, got, left, right, fl, fr, node, right_side)


def solution(mesh):
    in_specs = (P("narrow", None, None), P("narrow", None, None), P(), P("wide", None), P("wide"))
    out_specs = P("narrow", None, None)
    return jax.shard_map(
        per_device, mesh=mesh, in_specs=in_specs, out_specs=out_specs, check_vma=False
    )
```

```python
import functools
import math

import jax
import jax.numpy as jnp
from jax import lax
from jax.experimental import pallas as pl
from jax.experimental.pallas import tpu as pltpu
from jax.sharding import PartitionSpec as P

Z_HI, X_SIZE, Z_LO, Y_SIZE, CORES = 4, 4, 2, 4, 2
NT = (((1,), (1,)), ((), ()))
NN = (((1,), (0,)), ((), ()))


def in_hbm(value):
    return pltpu.with_memory_space_constraint(value, pltpu.HBM)


def grant(mib):
    return pltpu.CompilerParams(vmem_limit_bytes=mib << 20)


def pairs_of(move):
    out = []
    for z_hi in range(Z_HI):
        for x in range(X_SIZE):
            for z_lo in range(Z_LO):
                for y in range(Y_SIZE):
                    for core in range(CORES):
                        a, b, c, d, e = move(z_hi, x, z_lo, y, core)
                        there = (a % Z_HI) * X_SIZE + b % X_SIZE
                        block = ((c % Z_LO) * Y_SIZE + d % Y_SIZE) * CORES + e % CORES
                        here = (z_hi * X_SIZE + x) * 16 + (z_lo * Y_SIZE + y) * CORES + core
                        out.append((here, there * 16 + block))
    return out


def send(value, dz_hi=0, dx=0, dz_lo=0, dy=0, dcore=0):
    def move(z_hi, x, z_lo, y, core):
        return z_hi + dz_hi, x + dx, z_lo + dz_lo, y + dy, core + dcore

    return lax.ppermute(value, ("wide", "narrow"), pairs_of(move))


def leg_c(node_ref, ops, scratch):
    rows = ops.shape[0]
    for a in range(16):
        block = lax.dot_general(ops, node_ref[a], NT, preferred_element_type=jnp.float32)
        for c in range(2):
            scratch[c, pl.ds(a, rows, stride=16), :] = block[:, c * 128 : (c + 1) * 128]


def put_first(scratch, out_ref):
    for k in range(12):
        for c in range(2):
            value = scratch[c, k * 128 : (k + 1) * 128].astype(jnp.bfloat16)
            out_ref[k, 0, :, c * 128 : (c + 1) * 128] = value


def prep_kernel(node_hbm, legs_hbm, first_ref, cols_ref, ops_ref, node_ref, leg_a, tiles, wide_tiles, scratch, sems):
    wide, narrow = lax.axis_index("wide"), lax.axis_index("narrow")
    core = lax.rem(narrow, 2)
    columns = pl.ds(pl.multiple_of(wide * 16, 16), 16)
    fetch_a = pltpu.make_async_copy(legs_hbm.at[0], leg_a, sems.at[0])
    fetch_c = pltpu.make_async_copy(legs_hbm.at[2, :, columns, :], tiles, sems.at[1])
    fetch_node = pltpu.make_async_copy(node_hbm, node_ref, sems.at[2])
    fetch_a.start()
    fetch_c.start()
    fetch_node.start()
    lane = lax.broadcasted_iota(jnp.int32, (256, 128), 1) % 32
    source = (narrow - core) * 16 + jnp.where(lane < 16, core * 16 + lane, (1 - core) * 16 + lane - 16)
    row = lax.broadcasted_iota(jnp.int32, (256, 128), 0)
    pick = jnp.where(row == source, 1.0, 0.0).astype(jnp.bfloat16)
    fetch_a.wait()
    for i in range(12):
        block = lax.dot_general(leg_a[i], pick, NN, preferred_element_type=jnp.float32)
        block = block.astype(jnp.bfloat16)
        cols_ref[i, :256] = block
        cols_ref[i, 256:] = block
    fetch_c.wait()
    wide_tiles[...] = tiles[...].astype(jnp.float32)
    half = [wide_tiles[k, pl.ds(pl.multiple_of(core * 8, 8), 8), :] for k in range(12)]
    ops = jnp.concatenate(half, axis=0).astype(jnp.bfloat16)
    ops_ref[...] = ops
    fetch_node.wait()
    leg_c(node_ref, ops, scratch)
    put_first(scratch, first_ref)


def prep(node, leg_ops):
    return pl.pallas_call(
        prep_kernel,
        out_shape=[
            jax.ShapeDtypeStruct((12, 2, 128, 256), jnp.bfloat16),
            jax.ShapeDtypeStruct((12, 512, 128), jnp.bfloat16),
            jax.ShapeDtypeStruct((96, 256), jnp.bfloat16),
        ],
        grid=(1,),
        in_specs=[pl.BlockSpec(memory_space=pltpu.HBM)] * 2,
        out_specs=[
            pl.BlockSpec((12, 1, 128, 256), lambda g: (0, 0, 0, 0)),
            pl.BlockSpec((12, 512, 128), lambda g: (0, 0, 0)),
            pl.BlockSpec((96, 256), lambda g: (0, 0)),
        ],
        scratch_shapes=[
            pltpu.VMEM((16, 256, 256), jnp.bfloat16),
            pltpu.VMEM((12, 256, 256), jnp.bfloat16),
            pltpu.VMEM((12, 16, 256), jnp.bfloat16),
            pltpu.VMEM((12, 16, 256), jnp.float32),
            pltpu.VMEM((2, 1536, 128), jnp.float32),
            pltpu.SemaphoreType.DMA((3,)),
        ],
        compiler_params=grant(14),
        cost_estimate=pl.CostEstimate(flops=2 * 3072 * 256 * 300, bytes_accessed=6 << 20, transcendentals=0),
        name="prep",
    )(in_hbm(node), in_hbm(leg_ops))


def sibling_kernel(node_ref, ops_ref, first_ref, out_ref, scratch):
    del first_ref
    leg_c(node_ref, ops_ref[...], scratch)
    put_first(scratch, out_ref)


def add_sibling(node, ops, first):
    return pl.pallas_call(
        sibling_kernel,
        out_shape=jax.ShapeDtypeStruct((12, 2, 128, 256), jnp.bfloat16),
        grid=(1,),
        in_specs=[
            pl.BlockSpec((16, 256, 256), lambda g: (0, 0, 0)),
            pl.BlockSpec((96, 256), lambda g: (0, 0)),
            pl.BlockSpec(memory_space=pl.ANY),
        ],
        out_specs=pl.BlockSpec((12, 1, 128, 256), lambda g: (0, 1, 0, 0)),
        scratch_shapes=[pltpu.VMEM((2, 1536, 128), jnp.float32)],
        input_output_aliases={2: 0},
        compiler_params=grant(10),
        cost_estimate=pl.CostEstimate(flops=2 * 1536 * 65536, bytes_accessed=3 << 20, transcendentals=0),
        name="sibling",
    )(node, ops, first)


def table_kernel(index_ref, offset_ref, out_ref):
    shape = (16, 128)
    row, lane = lax.broadcasted_iota(jnp.int32, shape, 0), lax.broadcasted_iota(jnp.int32, shape, 1)
    value = jnp.zeros(shape, jnp.int32)
    for t in range(4):
        for m in range(4):
            entry = offset_ref[t] if m == 3 else index_ref[t, m]
            value = jnp.where(lane == t * 4 + m, entry, value)
    out_ref[...] = jnp.where(row == lax.axis_index("wide"), value, 0)


def own_rows(op_index, offsets):
    smem = pl.BlockSpec(memory_space=pltpu.SMEM)
    return pl.pallas_call(
        table_kernel,
        out_shape=jax.ShapeDtypeStruct((16, 128), jnp.int32),
        in_specs=[smem, smem],
        compiler_params=grant(1),
        name="own_rows",
    )(in_hbm(op_index), in_hbm(offsets))


def main_kernel(table, first_ref, legs_hbm, cols_ref, keep_ref, m1_ref, m2_ref, m3_ref, leg_b, second, a_abs, a_rel, sem):
    fetch = pltpu.make_async_copy(legs_hbm.at[1], leg_b, sem)
    fetch.start()
    narrow = lax.axis_index("narrow")
    lane = lax.broadcasted_iota(jnp.int32, (16, 128), 1) // 32

    def fill(g, carry):
        starts = []
        for s in range(4):
            start = pl.multiple_of(256 - 32 * table[g, s * 4 + 3], 32)
            starts.append((table[g, s * 4], start))
        for blk in range(16):
            value = None
            for s, (i, start) in enumerate(starts):
                part = cols_ref[i, pl.ds(start + 16 * blk, 16), :]
                value = part if value is None else jnp.where(lane == s, part, value)
            a_abs[g, pl.ds(16 * blk, 16), :] = value
        return carry

    lax.fori_loop(0, 16, fill, 0)
    core, z_lo = lax.rem(narrow, 2), narrow // 8
    y = lax.rem(narrow // 2, 4)
    for blk in range(16):
        dy, dz, dc = blk // 4, (blk // 2) % 2, blk % 2
        block = lax.rem(z_lo + dz, 2) * 8 + lax.rem(y + dy, 4) * 2 + lax.rem(core + dc, 2)
        source = pl.multiple_of(block * 16, 16)
        for g in range(16):
            a_rel[16 * blk : 16 * blk + 16, g * 128 : (g + 1) * 128] = a_abs[g, pl.ds(source, 16), :]

    fetch.wait()

    def step(g, carry):
        for s in range(4):
            j, k = table[g, s * 4 + 1], table[g, s * 4 + 2]
            lhs = first_ref[k].reshape(256, 256)
            value = lax.dot_general(lhs, leg_b[j], NT, preferred_element_type=jnp.float32)
            value = value.astype(jnp.bfloat16)
            for half in range(2):
                for q in range(8):
                    where = pl.multiple_of(g * 128 + s * 32 + half * 16, 16)
                    source = half * 128 + q * 16
                    second[q, pl.ds(where, 16), :] = value[source : source + 16]
        return carry

    lax.fori_loop(0, 16, step, 0)
    for q in range(8):
        value = lax.dot_general(a_rel[...], second[q], NN, preferred_element_type=jnp.float32)
        keep_ref[q] = value[:64]
        m1_ref[q] = value[64:128].astype(jnp.bfloat16)
        m2_ref[q] = value[128:192].astype(jnp.bfloat16)
        m3_ref[q] = value[192:].astype(jnp.bfloat16)


def main_of(table, first, leg_ops, cols):
    whole3 = lambda g, s: (0, 0, 0)
    return pl.pallas_call(
        main_kernel,
        out_shape=[jax.ShapeDtypeStruct((8, 64, 256), jnp.float32)]
        + [jax.ShapeDtypeStruct((8, 64, 256), jnp.bfloat16)] * 3,
        grid_spec=pltpu.PrefetchScalarGridSpec(
            num_scalar_prefetch=1,
            grid=(1,),
            in_specs=[
                pl.BlockSpec((12, 2, 128, 256), lambda g, s: (0, 0, 0, 0)),
                pl.BlockSpec(memory_space=pltpu.HBM),
                pl.BlockSpec((12, 512, 128), whole3),
            ],
            out_specs=[pl.BlockSpec((8, 64, 256), whole3)] * 4,
            scratch_shapes=[
                pltpu.VMEM((12, 256, 256), jnp.bfloat16),
                pltpu.VMEM((8, 2048, 256), jnp.bfloat16),
                pltpu.VMEM((16, 256, 128), jnp.bfloat16),
                pltpu.VMEM((256, 2048), jnp.bfloat16),
                pltpu.SemaphoreType.DMA(()),
            ],
        ),
        compiler_params=grant(28),
        cost_estimate=pl.CostEstimate(flops=128 * 2 * 256**3, bytes_accessed=8 << 20, transcendentals=0),
        name="two_legs",
    )(table, first, in_hbm(leg_ops), cols)


def y_kernel(keep_ref, r1_ref, r2_ref, r3_ref, keep_out, m01_ref, m10_ref, m11_ref):
    f32 = jnp.float32
    for q in range(8):
        value = keep_ref[q] + r1_ref[q].astype(f32) + r2_ref[q].astype(f32) + r3_ref[q].astype(f32)
        keep_out[q] = value[:16]
        m01_ref[q] = value[16:32].astype(jnp.bfloat16)
        m10_ref[q] = value[32:48].astype(jnp.bfloat16)
        m11_ref[q] = value[48:].astype(jnp.bfloat16)


def y_sum(keep, r1, r2, r3):
    return pl.pallas_call(
        y_kernel,
        out_shape=[jax.ShapeDtypeStruct((8, 16, 256), jnp.float32)]
        + [jax.ShapeDtypeStruct((8, 16, 256), jnp.bfloat16)] * 3,
        compiler_params=grant(6),
        name="sum_y",
    )(keep, r1, r2, r3)


def z_kernel(keep_ref, r01_ref, r10_ref, r11_ref, out_ref, scratch):
    f32 = jnp.float32
    core = lax.rem(lax.axis_index("narrow"), 2)
    for q in range(8):
        mine = keep_ref[q] + r10_ref[q].astype(f32)
        other = r01_ref[q].astype(f32) + r11_ref[q].astype(f32)
        low = jnp.where(core == 0, mine, other)
        high = jnp.where(core == 0, other, mine)
        for c in range(2):
            scratch[c, pl.ds(q, 16, stride=16), :] = low[:, c * 128 : (c + 1) * 128]
            scratch[c, pl.ds(8 + q, 16, stride=16), :] = high[:, c * 128 : (c + 1) * 128]
    for c in range(2):
        out_ref[:, c * 128 : (c + 1) * 128] = scratch[c].astype(jnp.bfloat16)


def z_sum(keep, r01, r10, r11):
    vmem = pl.BlockSpec(memory_space=pltpu.VMEM)
    return pl.pallas_call(
        z_kernel,
        out_shape=jax.ShapeDtypeStruct((256, 256), jnp.bfloat16),
        in_specs=[vmem] * 4,
        out_specs=vmem,
        scratch_shapes=[pltpu.VMEM((2, 256, 128), jnp.float32)],
        compiler_params=grant(3),
        name="sum_z",
    )(keep, r01, r10, r11)


def last_kernel(tau, n0, n2, l0, l2, r0, r2, fl, fr, f2, node_ref, side_ref, out_ref, sigma):
    f32 = jnp.float32
    wide = lax.axis_index("wide")
    z_hi, x = wide // 4, lax.rem(wide, 4)
    row = lax.broadcasted_iota(jnp.int32, (256, 256), 0)
    column = lax.broadcasted_iota(jnp.int32, (256, 256), 1)
    eye = jnp.where(row == column, 1.0, 0.0).astype(jnp.bfloat16)
    pieces = []
    for dx, near, far in ((0, n0, n2), (1, l0, l2), (3, r0, r2)):
        pieces += [(dx, 0, near, 0), (dx, 1, near, 1), (dx, 3, near, 2), (dx, 2, far, 0)]
    pieces += [(2, 0, fl, 0), (2, 1, fl, 1), (2, 3, fr, 0), (2, 2, f2, 0)]
    for r in range(ROWS):
        for dx, dz, ref, slot in pieces:
            w = lax.rem(z_hi - dz + 4, 4) * 4 + lax.rem(x - dx + 4, 4)
            place = pl.ds(pl.multiple_of(w * 16, 16), 16)
            sigma[r, place, :] = ref[slot, r * 16 : (r + 1) * 16]
    for r in range(ROWS):
        turned = lax.dot_general(eye, sigma[r], NT, preferred_element_type=f32)
        out_ref[r] = node_ref[r].astype(f32) + tau * (side_ref[r].astype(f32) - turned)


ROWS = 4


def last_of(tau, pieces, node, side):
    def piece(n):
        return pl.BlockSpec((n, ROWS * 16, 256), lambda r: (0, r, 0))

    row = pl.BlockSpec((ROWS, 256, 256), lambda r: (r, 0, 0))
    return pl.pallas_call(
        functools.partial(last_kernel, tau),
        out_shape=jax.ShapeDtypeStruct((16, 256, 256), jnp.float32),
        grid=(16 // ROWS,),
        in_specs=[piece(p.shape[0]) for p in pieces] + [row, row],
        out_specs=row,
        scratch_shapes=[pltpu.VMEM((ROWS, 256, 256), jnp.bfloat16)],
        compiler_params=grant(16),
        name="update",
    )(*pieces, node, side)


def per_device(node, right_side, leg_ops, op_index, offsets):
    tau = 0.5 / math.sqrt(op_index.shape[0] * lax.axis_size("wide"))
    table = own_rows(op_index, offsets)
    for axis in ("x", "z_hi"):
        table = table + sum(send(table, **{f"d{axis}": d}) for d in (1, 3, 2))
    sibling = send(node, dcore=1)
    first, cols, ops_c = prep(node, leg_ops)
    first = add_sibling(sibling, ops_c, first)
    keep, m1, m2, m3 = main_of(table, first, leg_ops, cols)
    r1, r3, r2 = send(m1, dy=1), send(m3, dy=3), send(m2, dy=2)
    keep, m01, m10, m11 = y_sum(keep, r1, r2, r3)
    r10, r11, r01 = send(m10, dz_lo=1), send(m11, dz_lo=1, dcore=1), send(m01, dcore=1)
    piece = z_sum(keep, r01, r10, r11)
    piece = piece[None]
    z1, z3 = send(piece, dz_hi=1), send(piece, dz_hi=3)
    near = jnp.concatenate([piece, z1, z3])
    l0, r0 = send(near, dx=1), send(near, dx=3)
    fa, fb = send(z1[:, :128], dz_hi=1), send(z3[:, 128:], dz_hi=3)
    far = jnp.concatenate([fa, fb], axis=1)
    l2, r2, f2 = send(far, dx=1), send(far, dx=3), send(far, dx=2)
    fl, fr = send(l0[:2], dx=1), send(r0[2:], dx=3)
    return last_of(tau, (near, far, l0, l2, r0, r2, fl, fr, f2), node, right_side)


def solution(mesh):
    in_specs = (P("narrow", None, None), P("narrow", None, None), P(), P("wide", None), P("wide"))
    out_specs = P("narrow", None, None)
    return jax.shard_map(
        per_device, mesh=mesh, in_specs=in_specs, out_specs=out_specs, check_vma=False
    )
```

```python
import functools
import math

import jax
import jax.numpy as jnp
from jax import lax
from jax.experimental import pallas as pl
from jax.experimental.pallas import tpu as pltpu
from jax.sharding import PartitionSpec as P

Z_HI, X_SIZE, Z_LO, Y_SIZE, CORES = 4, 4, 2, 4, 2
NT = (((1,), (1,)), ((), ()))
NN = (((1,), (0,)), ((), ()))


def in_hbm(value):
    return pltpu.with_memory_space_constraint(value, pltpu.HBM)


def grant(mib):
    return pltpu.CompilerParams(vmem_limit_bytes=mib << 20)


def pairs_of(move):
    out = []
    for z_hi in range(Z_HI):
        for x in range(X_SIZE):
            for z_lo in range(Z_LO):
                for y in range(Y_SIZE):
                    for core in range(CORES):
                        a, b, c, d, e = move(z_hi, x, z_lo, y, core)
                        there = (a % Z_HI) * X_SIZE + b % X_SIZE
                        block = ((c % Z_LO) * Y_SIZE + d % Y_SIZE) * CORES + e % CORES
                        here = (z_hi * X_SIZE + x) * 16 + (z_lo * Y_SIZE + y) * CORES + core
                        out.append((here, there * 16 + block))
    return out


def send(value, dz_hi=0, dx=0, dz_lo=0, dy=0, dcore=0):
    def move(z_hi, x, z_lo, y, core):
        return z_hi + dz_hi, x + dx, z_lo + dz_lo, y + dy, core + dcore

    return lax.ppermute(value, ("wide", "narrow"), pairs_of(move))


def leg_c(node_ref, ops, scratch):
    rows = ops.shape[0]
    for a in range(16):
        block = lax.dot_general(ops, node_ref[a], NT, preferred_element_type=jnp.float32)
        for c in range(2):
            scratch[c, pl.ds(a, rows, stride=16), :] = block[:, c * 128 : (c + 1) * 128]


def put_first(scratch, out_ref):
    for k in range(12):
        for c in range(2):
            value = scratch[c, k * 128 : (k + 1) * 128].astype(jnp.bfloat16)
            out_ref[k, 0, :, c * 128 : (c + 1) * 128] = value


def prep_kernel(node_hbm, legs_hbm, first_ref, cols_ref, ops_ref, node_ref, leg_a, tiles, wide_tiles, scratch, sems):
    wide, narrow = lax.axis_index("wide"), lax.axis_index("narrow")
    core = lax.rem(narrow, 2)
    columns = pl.ds(pl.multiple_of(wide * 16, 16), 16)
    fetch_a = pltpu.make_async_copy(legs_hbm.at[0], leg_a, sems.at[0])
    fetch_c = pltpu.make_async_copy(legs_hbm.at[2, :, columns, :], tiles, sems.at[1])
    fetch_node = pltpu.make_async_copy(node_hbm, node_ref, sems.at[2])
    fetch_a.start()
    fetch_c.start()
    fetch_node.start()
    lane = lax.broadcasted_iota(jnp.int32, (256, 128), 1) % 32
    source = (narrow - core) * 16 + jnp.where(lane < 16, core * 16 + lane, (1 - core) * 16 + lane - 16)
    row = lax.broadcasted_iota(jnp.int32, (256, 128), 0)
    pick = jnp.where(row == source, 1.0, 0.0).astype(jnp.bfloat16)
    fetch_a.wait()
    for i in range(12):
        block = lax.dot_general(leg_a[i], pick, NN, preferred_element_type=jnp.float32)
        block = block.astype(jnp.bfloat16)
        cols_ref[i, :256] = block
        cols_ref[i, 256:] = block
    fetch_c.wait()
    wide_tiles[...] = tiles[...].astype(jnp.float32)
    half = [wide_tiles[k, pl.ds(pl.multiple_of(core * 8, 8), 8), :] for k in range(12)]
    ops = jnp.concatenate(half, axis=0).astype(jnp.bfloat16)
    ops_ref[...] = ops
    fetch_node.wait()
    leg_c(node_ref, ops, scratch)
    put_first(scratch, first_ref)


def prep(node, leg_ops):
    return pl.pallas_call(
        prep_kernel,
        out_shape=[
            jax.ShapeDtypeStruct((12, 2, 128, 256), jnp.bfloat16),
            jax.ShapeDtypeStruct((12, 512, 128), jnp.bfloat16),
            jax.ShapeDtypeStruct((96, 256), jnp.bfloat16),
        ],
        grid=(1,),
        in_specs=[pl.BlockSpec(memory_space=pltpu.HBM)] * 2,
        out_specs=[
            pl.BlockSpec((12, 1, 128, 256), lambda g: (0, 0, 0, 0)),
            pl.BlockSpec((12, 512, 128), lambda g: (0, 0, 0)),
            pl.BlockSpec((96, 256), lambda g: (0, 0)),
        ],
        scratch_shapes=[
            pltpu.VMEM((16, 256, 256), jnp.bfloat16),
            pltpu.VMEM((12, 256, 256), jnp.bfloat16),
            pltpu.VMEM((12, 16, 256), jnp.bfloat16),
            pltpu.VMEM((12, 16, 256), jnp.float32),
            pltpu.VMEM((2, 1536, 128), jnp.float32),
            pltpu.SemaphoreType.DMA((3,)),
        ],
        compiler_params=grant(14),
        cost_estimate=pl.CostEstimate(flops=2 * 3072 * 256 * 300, bytes_accessed=6 << 20, transcendentals=0),
        name="prep",
    )(in_hbm(node), in_hbm(leg_ops))


def sibling_kernel(node_ref, ops_ref, first_ref, out_ref, scratch):
    del first_ref
    leg_c(node_ref, ops_ref[...], scratch)
    put_first(scratch, out_ref)


def add_sibling(node, ops, first):
    return pl.pallas_call(
        sibling_kernel,
        out_shape=jax.ShapeDtypeStruct((12, 2, 128, 256), jnp.bfloat16),
        grid=(1,),
        in_specs=[
            pl.BlockSpec((16, 256, 256), lambda g: (0, 0, 0)),
            pl.BlockSpec((96, 256), lambda g: (0, 0)),
            pl.BlockSpec(memory_space=pl.ANY),
        ],
        out_specs=pl.BlockSpec((12, 1, 128, 256), lambda g: (0, 1, 0, 0)),
        scratch_shapes=[pltpu.VMEM((2, 1536, 128), jnp.float32)],
        input_output_aliases={2: 0},
        compiler_params=grant(10),
        cost_estimate=pl.CostEstimate(flops=2 * 1536 * 65536, bytes_accessed=3 << 20, transcendentals=0),
        name="sibling",
    )(node, ops, first)


def table_kernel(index_ref, offset_ref, out_ref):
    shape = (16, 128)
    row, lane = lax.broadcasted_iota(jnp.int32, shape, 0), lax.broadcasted_iota(jnp.int32, shape, 1)
    value = jnp.zeros(shape, jnp.int32)
    for t in range(4):
        for m in range(4):
            entry = offset_ref[t] if m == 3 else index_ref[t, m]
            value = jnp.where(lane == t * 4 + m, entry, value)
    out_ref[...] = jnp.where(row == lax.axis_index("wide"), value, 0)


def own_rows(op_index, offsets):
    smem = pl.BlockSpec(memory_space=pltpu.SMEM)
    return pl.pallas_call(
        table_kernel,
        out_shape=jax.ShapeDtypeStruct((16, 128), jnp.int32),
        in_specs=[smem, smem],
        compiler_params=grant(1),
        name="own_rows",
    )(in_hbm(op_index), in_hbm(offsets))


def main_kernel(table, first_ref, legs_hbm, cols_ref, keep_ref, m1_ref, m2_ref, m3_ref, leg_b, second, a_abs, a_rel, sem):
    fetch = pltpu.make_async_copy(legs_hbm.at[1], leg_b, sem)
    fetch.start()
    narrow = lax.axis_index("narrow")
    lane = lax.broadcasted_iota(jnp.int32, (16, 128), 1) // 32

    def fill(g, carry):
        starts = []
        for s in range(4):
            start = pl.multiple_of(256 - 32 * table[g, s * 4 + 3], 32)
            starts.append((table[g, s * 4], start))
        for blk in range(16):
            value = None
            for s, (i, start) in enumerate(starts):
                part = cols_ref[i, pl.ds(start + 16 * blk, 16), :]
                value = part if value is None else jnp.where(lane == s, part, value)
            a_abs[g, pl.ds(16 * blk, 16), :] = value
        return carry

    lax.fori_loop(0, 16, fill, 0)
    core, z_lo = lax.rem(narrow, 2), narrow // 8
    y = lax.rem(narrow // 2, 4)
    for blk in range(16):
        dy, dz, dc = blk // 4, (blk // 2) % 2, blk % 2
        block = lax.rem(z_lo + dz, 2) * 8 + lax.rem(y + dy, 4) * 2 + lax.rem(core + dc, 2)
        source = pl.multiple_of(block * 16, 16)
        for g in range(16):
            a_rel[16 * blk : 16 * blk + 16, g * 128 : (g + 1) * 128] = a_abs[g, pl.ds(source, 16), :]

    fetch.wait()

    def step(g, carry):
        for s in range(4):
            j, k = table[g, s * 4 + 1], table[g, s * 4 + 2]
            lhs = first_ref[k].reshape(256, 256)
            value = lax.dot_general(lhs, leg_b[j], NT, preferred_element_type=jnp.float32)
            value = value.astype(jnp.bfloat16)
            for half in range(2):
                for q in range(8):
                    where = pl.multiple_of(g * 128 + s * 32 + half * 16, 16)
                    source = half * 128 + q * 16
                    second[q, pl.ds(where, 16), :] = value[source : source + 16]
        return carry

    lax.fori_loop(0, 16, step, 0, unroll=True)
    for q in range(8):
        value = lax.dot_general(a_rel[...], second[q], NN, preferred_element_type=jnp.float32)
        keep_ref[q] = value[:64]
        m1_ref[q] = value[64:128].astype(jnp.bfloat16)
        m2_ref[q] = value[128:192].astype(jnp.bfloat16)
        m3_ref[q] = value[192:].astype(jnp.bfloat16)


def main_of(table, first, leg_ops, cols):
    whole3 = lambda g, s: (0, 0, 0)
    return pl.pallas_call(
        main_kernel,
        out_shape=[jax.ShapeDtypeStruct((8, 64, 256), jnp.float32)]
        + [jax.ShapeDtypeStruct((8, 64, 256), jnp.bfloat16)] * 3,
        grid_spec=pltpu.PrefetchScalarGridSpec(
            num_scalar_prefetch=1,
            grid=(1,),
            in_specs=[
                pl.BlockSpec((12, 2, 128, 256), lambda g, s: (0, 0, 0, 0)),
                pl.BlockSpec(memory_space=pltpu.HBM),
                pl.BlockSpec((12, 512, 128), whole3),
            ],
            out_specs=[pl.BlockSpec((8, 64, 256), whole3)] * 4,
            scratch_shapes=[
                pltpu.VMEM((12, 256, 256), jnp.bfloat16),
                pltpu.VMEM((8, 2048, 256), jnp.bfloat16),
                pltpu.VMEM((16, 256, 128), jnp.bfloat16),
                pltpu.VMEM((256, 2048), jnp.bfloat16),
                pltpu.SemaphoreType.DMA(()),
            ],
        ),
        compiler_params=grant(28),
        cost_estimate=pl.CostEstimate(flops=128 * 2 * 256**3, bytes_accessed=8 << 20, transcendentals=0),
        name="two_legs",
    )(table, first, in_hbm(leg_ops), cols)


def y_kernel(keep_ref, r1_ref, r2_ref, r3_ref, keep_out, m01_ref, m10_ref, m11_ref):
    f32 = jnp.float32
    for q in range(8):
        value = keep_ref[q] + r1_ref[q].astype(f32) + r2_ref[q].astype(f32) + r3_ref[q].astype(f32)
        keep_out[q] = value[:16]
        m01_ref[q] = value[16:32].astype(jnp.bfloat16)
        m10_ref[q] = value[32:48].astype(jnp.bfloat16)
        m11_ref[q] = value[48:].astype(jnp.bfloat16)


def y_sum(keep, r1, r2, r3):
    return pl.pallas_call(
        y_kernel,
        out_shape=[jax.ShapeDtypeStruct((8, 16, 256), jnp.float32)]
        + [jax.ShapeDtypeStruct((8, 16, 256), jnp.bfloat16)] * 3,
        compiler_params=grant(6),
        name="sum_y",
    )(keep, r1, r2, r3)


def z_kernel(keep_ref, r01_ref, r10_ref, r11_ref, out_ref, scratch):
    f32 = jnp.float32
    core = lax.rem(lax.axis_index("narrow"), 2)
    for q in range(8):
        mine = keep_ref[q] + r10_ref[q].astype(f32)
        other = r01_ref[q].astype(f32) + r11_ref[q].astype(f32)
        low = jnp.where(core == 0, mine, other)
        high = jnp.where(core == 0, other, mine)
        for c in range(2):
            scratch[c, pl.ds(q, 16, stride=16), :] = low[:, c * 128 : (c + 1) * 128]
            scratch[c, pl.ds(8 + q, 16, stride=16), :] = high[:, c * 128 : (c + 1) * 128]
    for c in range(2):
        out_ref[:, c * 128 : (c + 1) * 128] = scratch[c].astype(jnp.bfloat16)


def z_sum(keep, r01, r10, r11):
    vmem = pl.BlockSpec(memory_space=pltpu.VMEM)
    return pl.pallas_call(
        z_kernel,
        out_shape=jax.ShapeDtypeStruct((256, 256), jnp.bfloat16),
        in_specs=[vmem] * 4,
        out_specs=vmem,
        scratch_shapes=[pltpu.VMEM((2, 256, 128), jnp.float32)],
        compiler_params=grant(3),
        name="sum_z",
    )(keep, r01, r10, r11)


def last_kernel(tau, n0, l0, r0, n1, l1, r1, n2, l2, r2, fl, fr, f2, node_ref, side_ref, out_hbm, sigma, out, sems):
    f32 = jnp.float32
    wide = lax.axis_index("wide")
    z_hi, x = wide // 4, lax.rem(wide, 4)
    row = lax.broadcasted_iota(jnp.int32, (256, 256), 0)
    column = lax.broadcasted_iota(jnp.int32, (256, 256), 1)
    eye = jnp.where(row == column, 1.0, 0.0).astype(jnp.bfloat16)
    pieces = []
    for dx, (own, near, far) in zip((0, 1, 3), ((n0, n1, n2), (l0, l1, l2), (r0, r1, r2))):
        pieces += [(dx, 0, own, 0), (dx, 1, near, 0), (dx, 3, near, 1), (dx, 2, far, 0)]
    pieces += [(2, 0, fl, 0), (2, 1, fl, 1), (2, 3, fr, 0), (2, 2, f2, 0)]
    places = []
    for dx, dz, _, _ in pieces:
        w = lax.rem(z_hi - dz + 4, 4) * 4 + lax.rem(x - dx + 4, 4)
        places.append(pl.ds(pl.multiple_of(w * 16, 16), 16))
    for r in range(16):
        for place, (_, _, ref, slot) in zip(places, pieces):
            sigma[r, place, :] = ref[slot, r * 16 : (r + 1) * 16]
        turned = lax.dot_general(eye, sigma[r], NT, preferred_element_type=f32)
        out[r] = node_ref[r].astype(f32) + tau * (side_ref[r].astype(f32) - turned)
        pltpu.make_async_copy(out.at[r], out_hbm.at[r], sems.at[r]).start()
    for r in range(16):
        pltpu.make_async_copy(out.at[r], out_hbm.at[r], sems.at[r]).wait()


def last_of(tau, pieces, node, side):
    return pl.pallas_call(
        functools.partial(last_kernel, tau),
        out_shape=jax.ShapeDtypeStruct((16, 256, 256), jnp.float32),
        in_specs=[pl.BlockSpec(memory_space=pltpu.VMEM)] * (len(pieces) + 2),
        out_specs=pl.BlockSpec(memory_space=pltpu.HBM),
        scratch_shapes=[
            pltpu.VMEM((16, 256, 256), jnp.bfloat16),
            pltpu.VMEM((16, 256, 256), jnp.float32),
            pltpu.SemaphoreType.DMA((16,)),
        ],
        compiler_params=grant(16),
        name="update",
    )(*pieces, node, side)


def per_device(node, right_side, leg_ops, op_index, offsets):
    tau = 0.5 / math.sqrt(op_index.shape[0] * lax.axis_size("wide"))
    table = own_rows(op_index, offsets)
    for axis in ("x", "z_hi"):
        table = table + sum(send(table, **{f"d{axis}": d}) for d in (1, 3, 2))
    sibling = send(node, dcore=1)
    first, cols, ops_c = prep(node, leg_ops)
    first = add_sibling(sibling, ops_c, first)
    keep, m1, m2, m3 = main_of(table, first, leg_ops, cols)
    r1, r3, r2 = send(m1, dy=1), send(m3, dy=3), send(m2, dy=2)
    keep, m01, m10, m11 = y_sum(keep, r1, r2, r3)
    r10, r11, r01 = send(m10, dz_lo=1), send(m11, dz_lo=1, dcore=1), send(m01, dcore=1)
    piece = z_sum(keep, r01, r10, r11)
    piece = piece[None]
    z1, z3 = send(piece, dz_hi=1), send(piece, dz_hi=3)
    l0, r0 = send(piece, dx=1), send(piece, dx=3)
    fa = send(z1[:, :128], dz_hi=1)
    near = jnp.concatenate([z1, z3])
    l1, r1 = send(near, dx=1), send(near, dx=3)
    fb = send(z3[:, 128:], dz_hi=3)
    far = jnp.concatenate([fa, fb], axis=1)
    l2, r2, f2 = send(far, dx=1), send(far, dx=3), send(far, dx=2)
    fl, fr = send(jnp.concatenate([l0, l1[:1]]), dx=1), send(r1[1:], dx=3)
    pieces = (piece, l0, r0, near, l1, r1, far, l2, r2, fl, fr, f2)
    return last_of(tau, pieces, node, right_side)


def solution(mesh):
    in_specs = (P("narrow", None, None), P("narrow", None, None), P(), P("wide", None), P("wide"))
    out_specs = P("narrow", None, None)
    return jax.shard_map(
        per_device, mesh=mesh, in_specs=in_specs, out_specs=out_specs, check_vma=False
    )
```

```python
import functools
import math

import jax
import jax.numpy as jnp
from jax import lax
from jax.experimental import pallas as pl
from jax.experimental.pallas import tpu as pltpu
from jax.sharding import PartitionSpec as P

Z_HI, X_SIZE, Z_LO, Y_SIZE, CORES = 4, 4, 2, 4, 2
NT = (((1,), (1,)), ((), ()))
NN = (((1,), (0,)), ((), ()))


def in_hbm(value):
    return pltpu.with_memory_space_constraint(value, pltpu.HBM)


def grant(mib):
    return pltpu.CompilerParams(vmem_limit_bytes=mib << 20)


def pairs_of(move):
    out = []
    for z_hi in range(Z_HI):
        for x in range(X_SIZE):
            for z_lo in range(Z_LO):
                for y in range(Y_SIZE):
                    for core in range(CORES):
                        a, b, c, d, e = move(z_hi, x, z_lo, y, core)
                        there = (a % Z_HI) * X_SIZE + b % X_SIZE
                        block = ((c % Z_LO) * Y_SIZE + d % Y_SIZE) * CORES + e % CORES
                        here = (z_hi * X_SIZE + x) * 16 + (z_lo * Y_SIZE + y) * CORES + core
                        out.append((here, there * 16 + block))
    return out


def send(value, dz_hi=0, dx=0, dz_lo=0, dy=0, dcore=0):
    def move(z_hi, x, z_lo, y, core):
        return z_hi + dz_hi, x + dx, z_lo + dz_lo, y + dy, core + dcore

    return lax.ppermute(value, ("wide", "narrow"), pairs_of(move))


def leg_c(node_ref, ops, scratch):
    rows = ops.shape[0]
    for a in range(16):
        block = lax.dot_general(ops, node_ref[a], NT, preferred_element_type=jnp.float32)
        for c in range(2):
            scratch[c, pl.ds(a, rows, stride=16), :] = block[:, c * 128 : (c + 1) * 128]


def put_first(scratch, out_ref):
    for k in range(12):
        for c in range(2):
            value = scratch[c, k * 128 : (k + 1) * 128].astype(jnp.bfloat16)
            out_ref[k, 0, :, c * 128 : (c + 1) * 128] = value


def prep_kernel(node_hbm, legs_hbm, first_ref, cols_ref, ops_ref, node_ref, leg_a, tiles, wide_tiles, scratch, sems):
    wide, narrow = lax.axis_index("wide"), lax.axis_index("narrow")
    core = lax.rem(narrow, 2)
    columns = pl.ds(pl.multiple_of(wide * 16, 16), 16)
    fetch_a = [
        pltpu.make_async_copy(legs_hbm.at[0, pl.ds(3 * n, 3)], leg_a.at[pl.ds(3 * n, 3)], sems.at[2 + n])
        for n in range(4)
    ]
    fetch_c = pltpu.make_async_copy(legs_hbm.at[2, :, columns, :], tiles, sems.at[0])
    fetch_node = pltpu.make_async_copy(node_hbm, node_ref, sems.at[1])
    for copy in fetch_a:
        copy.start()
    fetch_c.start()
    fetch_node.start()
    lane = lax.broadcasted_iota(jnp.int32, (256, 128), 1) % 32
    source = (narrow - core) * 16 + jnp.where(lane < 16, core * 16 + lane, (1 - core) * 16 + lane - 16)
    row = lax.broadcasted_iota(jnp.int32, (256, 128), 0)
    pick = jnp.where(row == source, 1.0, 0.0).astype(jnp.bfloat16)
    for i in range(12):
        if i % 3 == 0:
            fetch_a[i // 3].wait()
        block = lax.dot_general(leg_a[i], pick, NN, preferred_element_type=jnp.float32)
        block = block.astype(jnp.bfloat16)
        cols_ref[i, :256] = block
        cols_ref[i, 256:] = block
    fetch_c.wait()
    wide_tiles[...] = tiles[...].astype(jnp.float32)
    half = [wide_tiles[k, pl.ds(pl.multiple_of(core * 8, 8), 8), :] for k in range(12)]
    ops = jnp.concatenate(half, axis=0).astype(jnp.bfloat16)
    ops_ref[...] = ops
    fetch_node.wait()
    leg_c(node_ref, ops, scratch)
    put_first(scratch, first_ref)


def prep(node, leg_ops):
    return pl.pallas_call(
        prep_kernel,
        out_shape=[
            jax.ShapeDtypeStruct((12, 2, 128, 256), jnp.bfloat16),
            jax.ShapeDtypeStruct((12, 512, 128), jnp.bfloat16),
            jax.ShapeDtypeStruct((96, 256), jnp.bfloat16),
        ],
        grid=(1,),
        in_specs=[pl.BlockSpec(memory_space=pltpu.HBM)] * 2,
        out_specs=[
            pl.BlockSpec((12, 1, 128, 256), lambda g: (0, 0, 0, 0)),
            pl.BlockSpec((12, 512, 128), lambda g: (0, 0, 0)),
            pl.BlockSpec((96, 256), lambda g: (0, 0)),
        ],
        scratch_shapes=[
            pltpu.VMEM((16, 256, 256), jnp.bfloat16),
            pltpu.VMEM((12, 256, 256), jnp.bfloat16),
            pltpu.VMEM((12, 16, 256), jnp.bfloat16),
            pltpu.VMEM((12, 16, 256), jnp.float32),
            pltpu.VMEM((2, 1536, 128), jnp.float32),
            pltpu.SemaphoreType.DMA((6,)),
        ],
        compiler_params=grant(14),
        cost_estimate=pl.CostEstimate(flops=2 * 3072 * 256 * 300, bytes_accessed=6 << 20, transcendentals=0),
        name="prep",
    )(in_hbm(node), in_hbm(leg_ops))


def sibling_kernel(node_ref, ops_ref, first_ref, out_ref, scratch):
    del first_ref
    leg_c(node_ref, ops_ref[...], scratch)
    put_first(scratch, out_ref)


def add_sibling(node, ops, first):
    return pl.pallas_call(
        sibling_kernel,
        out_shape=jax.ShapeDtypeStruct((12, 2, 128, 256), jnp.bfloat16),
        grid=(1,),
        in_specs=[
            pl.BlockSpec((16, 256, 256), lambda g: (0, 0, 0)),
            pl.BlockSpec((96, 256), lambda g: (0, 0)),
            pl.BlockSpec(memory_space=pl.ANY),
        ],
        out_specs=pl.BlockSpec((12, 1, 128, 256), lambda g: (0, 1, 0, 0)),
        scratch_shapes=[pltpu.VMEM((2, 1536, 128), jnp.float32)],
        input_output_aliases={2: 0},
        compiler_params=grant(10),
        cost_estimate=pl.CostEstimate(flops=2 * 1536 * 65536, bytes_accessed=3 << 20, transcendentals=0),
        name="sibling",
    )(node, ops, first)


def table_kernel(index_ref, offset_ref, out_ref):
    shape = (16, 128)
    row, lane = lax.broadcasted_iota(jnp.int32, shape, 0), lax.broadcasted_iota(jnp.int32, shape, 1)
    value = jnp.zeros(shape, jnp.int32)
    for t in range(4):
        for m in range(4):
            entry = offset_ref[t] if m == 3 else index_ref[t, m]
            value = jnp.where(lane == t * 4 + m, entry, value)
    out_ref[...] = jnp.where(row == lax.axis_index("wide"), value, 0)


def own_rows(op_index, offsets):
    smem = pl.BlockSpec(memory_space=pltpu.SMEM)
    return pl.pallas_call(
        table_kernel,
        out_shape=jax.ShapeDtypeStruct((16, 128), jnp.int32),
        in_specs=[smem, smem],
        compiler_params=grant(1),
        name="own_rows",
    )(in_hbm(op_index), in_hbm(offsets))


def main_kernel(table, first_ref, legs_hbm, cols_ref, second, a_own, m1_ref, m2_ref, m3_ref, leg_b, a_abs, a_rel, sem):
    fetch = pltpu.make_async_copy(legs_hbm.at[1], leg_b, sem)
    fetch.start()
    narrow = lax.axis_index("narrow")
    lane = lax.broadcasted_iota(jnp.int32, (16, 128), 1) // 32

    def fill(g, carry):
        starts = []
        for s in range(4):
            start = pl.multiple_of(256 - 32 * table[g, s * 4 + 3], 32)
            starts.append((table[g, s * 4], start))
        for blk in range(16):
            value = None
            for s, (i, start) in enumerate(starts):
                part = cols_ref[i, pl.ds(start + 16 * blk, 16), :]
                value = part if value is None else jnp.where(lane == s, part, value)
            a_abs[g, pl.ds(16 * blk, 16), :] = value
        return carry

    lax.fori_loop(0, 16, fill, 0)
    core, z_lo = lax.rem(narrow, 2), narrow // 8
    y = lax.rem(narrow // 2, 4)
    for blk in range(16):
        dy, dz, dc = blk // 4, (blk // 2) % 2, blk % 2
        block = lax.rem(z_lo + dz, 2) * 8 + lax.rem(y + dy, 4) * 2 + lax.rem(core + dc, 2)
        source = pl.multiple_of(block * 16, 16)
        for g in range(16):
            rows = a_own if blk < 4 else a_rel
            row = 16 * (blk % 4 if blk < 4 else blk - 4)
            rows[row : row + 16, g * 128 : (g + 1) * 128] = a_abs[g, pl.ds(source, 16), :]

    fetch.wait()

    def step(g, carry):
        for s in range(4):
            j, k = table[g, s * 4 + 1], table[g, s * 4 + 2]
            lhs = first_ref[k].reshape(256, 256)
            value = lax.dot_general(lhs, leg_b[j], NT, preferred_element_type=jnp.float32)
            value = value.astype(jnp.bfloat16)
            for half in range(2):
                for q in range(8):
                    where = pl.multiple_of(g * 128 + s * 32 + half * 16, 16)
                    source = half * 128 + q * 16
                    second[q, pl.ds(where, 16), :] = value[source : source + 16]
        return carry

    lax.fori_loop(0, 16, step, 0, unroll=True)
    for q in range(8):
        value = lax.dot_general(a_rel[...], second[q], NN, preferred_element_type=jnp.float32)
        m1_ref[q] = value[:64].astype(jnp.bfloat16)
        m2_ref[q] = value[64:128].astype(jnp.bfloat16)
        m3_ref[q] = value[128:].astype(jnp.bfloat16)


def keep_kernel(second, a_own, keep_ref):
    for q in range(8):
        keep_ref[q] = lax.dot_general(a_own[...], second[q], NN, preferred_element_type=jnp.float32)


def keep_of(second, a_own):
    return pl.pallas_call(
        keep_kernel,
        out_shape=jax.ShapeDtypeStruct((8, 64, 256), jnp.float32),
        in_specs=[pl.BlockSpec(memory_space=pltpu.VMEM)] * 2,
        out_specs=pl.BlockSpec(memory_space=pltpu.VMEM),
        compiler_params=grant(4),
        cost_estimate=pl.CostEstimate(flops=2 * 64 * 2048 * 2048, bytes_accessed=9 << 20, transcendentals=0),
        name="own_target",
    )(second, a_own)


def main_of(table, first, leg_ops, cols):
    whole3 = lambda g, s: (0, 0, 0)
    return pl.pallas_call(
        main_kernel,
        out_shape=[jax.ShapeDtypeStruct((8, 2048, 256), jnp.bfloat16), jax.ShapeDtypeStruct((64, 2048), jnp.bfloat16)]
        + [jax.ShapeDtypeStruct((8, 64, 256), jnp.bfloat16)] * 3,
        grid_spec=pltpu.PrefetchScalarGridSpec(
            num_scalar_prefetch=1,
            grid=(1,),
            in_specs=[
                pl.BlockSpec((12, 2, 128, 256), lambda g, s: (0, 0, 0, 0)),
                pl.BlockSpec(memory_space=pltpu.HBM),
                pl.BlockSpec((12, 512, 128), whole3),
            ],
            out_specs=[pl.BlockSpec(memory_space=pltpu.VMEM)] * 5,
            scratch_shapes=[
                pltpu.VMEM((12, 256, 256), jnp.bfloat16),
                pltpu.VMEM((16, 256, 128), jnp.bfloat16),
                pltpu.VMEM((192, 2048), jnp.bfloat16),
                pltpu.SemaphoreType.DMA(()),
            ],
        ),
        compiler_params=grant(28),
        cost_estimate=pl.CostEstimate(flops=128 * 2 * 256**3, bytes_accessed=8 << 20, transcendentals=0),
        name="two_legs",
    )(table, first, in_hbm(leg_ops), cols)


def y_kernel(keep_ref, r1_ref, r2_ref, r3_ref, keep_out, m01_ref, m10_ref, m11_ref):
    f32 = jnp.float32
    for q in range(8):
        value = keep_ref[q] + r1_ref[q].astype(f32) + r2_ref[q].astype(f32) + r3_ref[q].astype(f32)
        keep_out[q] = value[:16]
        m01_ref[q] = value[16:32].astype(jnp.bfloat16)
        m10_ref[q] = value[32:48].astype(jnp.bfloat16)
        m11_ref[q] = value[48:].astype(jnp.bfloat16)


def y_sum(keep, r1, r2, r3):
    return pl.pallas_call(
        y_kernel,
        out_shape=[jax.ShapeDtypeStruct((8, 16, 256), jnp.float32)]
        + [jax.ShapeDtypeStruct((8, 16, 256), jnp.bfloat16)] * 3,
        compiler_params=grant(6),
        name="sum_y",
    )(keep, r1, r2, r3)


def z_kernel(keep_ref, r01_ref, r10_ref, r11_ref, out_ref, scratch):
    f32 = jnp.float32
    core = lax.rem(lax.axis_index("narrow"), 2)
    for q in range(8):
        mine = keep_ref[q] + r10_ref[q].astype(f32)
        other = r01_ref[q].astype(f32) + r11_ref[q].astype(f32)
        low = jnp.where(core == 0, mine, other)
        high = jnp.where(core == 0, other, mine)
        for c in range(2):
            scratch[c, pl.ds(q, 16, stride=16), :] = low[:, c * 128 : (c + 1) * 128]
            scratch[c, pl.ds(8 + q, 16, stride=16), :] = high[:, c * 128 : (c + 1) * 128]
    for c in range(2):
        out_ref[:, c * 128 : (c + 1) * 128] = scratch[c].astype(jnp.bfloat16)


def z_sum(keep, r01, r10, r11):
    vmem = pl.BlockSpec(memory_space=pltpu.VMEM)
    return pl.pallas_call(
        z_kernel,
        out_shape=jax.ShapeDtypeStruct((256, 256), jnp.bfloat16),
        in_specs=[vmem] * 4,
        out_specs=vmem,
        scratch_shapes=[pltpu.VMEM((2, 256, 128), jnp.float32)],
        compiler_params=grant(3),
        name="sum_z",
    )(keep, r01, r10, r11)


def last_kernel(tau, n0, l0, r0, n1, l1, r1, n2, f0, fl, fr, f2, node_ref, side_ref, out_hbm, sigma, out, sems):
    f32 = jnp.float32
    wide = lax.axis_index("wide")
    z_hi, x = wide // 4, lax.rem(wide, 4)
    row = lax.broadcasted_iota(jnp.int32, (256, 256), 0)
    column = lax.broadcasted_iota(jnp.int32, (256, 256), 1)
    eye = jnp.where(row == column, 1.0, 0.0).astype(jnp.bfloat16)
    pieces = []
    for dx, own, near, (far, slot) in ((0, n0, n1, (n2, 0)), (1, l0, l1, (fl, 1)), (3, r0, r1, (fr, 1))):
        pieces += [(dx, 0, own, 0), (dx, 1, near, 0), (dx, 3, near, 1), (dx, 2, far, slot)]
    pieces += [(2, 0, f0, 0), (2, 1, fl, 0), (2, 3, fr, 0), (2, 2, f2, 0)]
    places = []
    for dx, dz, _, _ in pieces:
        w = lax.rem(z_hi - dz + 4, 4) * 4 + lax.rem(x - dx + 4, 4)
        places.append(pl.ds(pl.multiple_of(w * 16, 16), 16))
    for r in range(16):
        for place, (_, _, ref, slot) in zip(places, pieces):
            sigma[r, place, :] = ref[slot, r * 16 : (r + 1) * 16]
        turned = lax.dot_general(eye, sigma[r], NT, preferred_element_type=f32)
        out[r] = node_ref[r].astype(f32) + tau * (side_ref[r].astype(f32) - turned)
        pltpu.make_async_copy(out.at[r], out_hbm.at[r], sems.at[r]).start()
    for r in range(16):
        pltpu.make_async_copy(out.at[r], out_hbm.at[r], sems.at[r]).wait()


def last_of(tau, pieces, node, side):
    return pl.pallas_call(
        functools.partial(last_kernel, tau),
        out_shape=jax.ShapeDtypeStruct((16, 256, 256), jnp.float32),
        in_specs=[pl.BlockSpec(memory_space=pltpu.VMEM)] * (len(pieces) + 2),
        out_specs=pl.BlockSpec(memory_space=pltpu.HBM),
        scratch_shapes=[
            pltpu.VMEM((16, 256, 256), jnp.bfloat16),
            pltpu.VMEM((16, 256, 256), jnp.float32),
            pltpu.SemaphoreType.DMA((16,)),
        ],
        compiler_params=grant(16),
        name="update",
    )(*pieces, node, side)


def per_device(node, right_side, leg_ops, op_index, offsets):
    tau = 0.5 / math.sqrt(op_index.shape[0] * lax.axis_size("wide"))
    table = own_rows(op_index, offsets)
    for axis in ("x", "z_hi"):
        table = table + sum(send(table, **{f"d{axis}": d}) for d in (1, 3, 2))
    sibling = send(node, dcore=1)
    first, cols, ops_c = prep(node, leg_ops)
    first = add_sibling(sibling, ops_c, first)
    second, a_own, m1, m2, m3 = main_of(table, first, leg_ops, cols)
    r1, r3, r2 = send(m1, dy=1), send(m3, dy=3), send(m2, dy=2)
    keep = keep_of(second, a_own)
    keep, m01, m10, m11 = y_sum(keep, r1, r2, r3)
    r10, r11 = send(m10, dz_lo=1), send(m11, dz_lo=1, dcore=1)
    r01 = send(m01, dcore=1)
    piece = z_sum(keep, r01, r10, r11)
    piece = piece[None]
    z1, z3 = send(piece, dz_hi=1), send(piece, dz_hi=3)
    l0, r0 = send(piece, dx=1), send(piece, dx=3)
    fa = send(z1[:, :128], dz_hi=1)
    near = jnp.concatenate([z1, z3])
    l1, r1 = send(near, dx=1), send(near, dx=3)
    fb = send(z3[:, 128:], dz_hi=3)
    f0 = send(l0, dx=1)
    far = jnp.concatenate([fa, fb], axis=1)
    fl = send(jnp.concatenate([l1[:1], far]), dx=1)
    fr = send(jnp.concatenate([r1[1:], far]), dx=3)
    f2 = send(far, dx=2)
    pieces = (piece, l0, r0, near, l1, r1, far, f0, fl, fr, f2)
    return last_of(tau, pieces, node, right_side)


def solution(mesh):
    in_specs = (P("narrow", None, None), P("narrow", None, None), P(), P("wide", None), P("wide"))
    out_specs = P("narrow", None, None)
    return jax.shard_map(
        per_device, mesh=mesh, in_specs=in_specs, out_specs=out_specs, check_vma=False
    )
```

```python
import functools
import math

import jax
import jax.numpy as jnp
from jax import lax
from jax.experimental import pallas as pl
from jax.experimental.pallas import tpu as pltpu
from jax.sharding import PartitionSpec as P

Z_HI, X_SIZE, Z_LO, Y_SIZE, CORES = 4, 4, 2, 4, 2
NT = (((1,), (1,)), ((), ()))
NN = (((1,), (0,)), ((), ()))


def in_hbm(value):
    return pltpu.with_memory_space_constraint(value, pltpu.HBM)


def grant(mib):
    return pltpu.CompilerParams(vmem_limit_bytes=mib << 20)


def pairs_of(move):
    out = []
    for z_hi in range(Z_HI):
        for x in range(X_SIZE):
            for z_lo in range(Z_LO):
                for y in range(Y_SIZE):
                    for core in range(CORES):
                        a, b, c, d, e = move(z_hi, x, z_lo, y, core)
                        there = (a % Z_HI) * X_SIZE + b % X_SIZE
                        block = ((c % Z_LO) * Y_SIZE + d % Y_SIZE) * CORES + e % CORES
                        here = (z_hi * X_SIZE + x) * 16 + (z_lo * Y_SIZE + y) * CORES + core
                        out.append((here, there * 16 + block))
    return out


def send(value, dz_hi=0, dx=0, dz_lo=0, dy=0, dcore=0):
    def move(z_hi, x, z_lo, y, core):
        return z_hi + dz_hi, x + dx, z_lo + dz_lo, y + dy, core + dcore

    return lax.ppermute(value, ("wide", "narrow"), pairs_of(move))


def leg_c(node_ref, ops, scratch):
    rows = ops.shape[0]
    for a in range(16):
        block = lax.dot_general(ops, node_ref[a], NT, preferred_element_type=jnp.float32)
        for c in range(2):
            scratch[c, pl.ds(a, rows, stride=16), :] = block[:, c * 128 : (c + 1) * 128]


def put_first(scratch, out_ref, half):
    for k in range(12):
        for c in range(2):
            value = scratch[c, k * 128 : (k + 1) * 128].astype(jnp.bfloat16)
            out_ref[k, half, :, c * 128 : (c + 1) * 128] = value


def prep_kernel(node_hbm, legs_hbm, first_ref, cols_ref, ops_ref, node_ref, leg_a, tiles, wide_tiles, scratch, sems):
    wide, narrow = lax.axis_index("wide"), lax.axis_index("narrow")
    core = lax.rem(narrow, 2)
    columns = pl.ds(pl.multiple_of(wide * 16, 16), 16)
    fetch_a = [
        pltpu.make_async_copy(legs_hbm.at[0, pl.ds(3 * n, 3)], leg_a.at[pl.ds(3 * n, 3)], sems.at[2 + n])
        for n in range(4)
    ]
    fetch_c = pltpu.make_async_copy(legs_hbm.at[2, :, columns, :], tiles, sems.at[0])
    fetch_node = pltpu.make_async_copy(node_hbm, node_ref, sems.at[1])
    for copy in fetch_a:
        copy.start()
    fetch_c.start()
    fetch_node.start()
    lane = lax.broadcasted_iota(jnp.int32, (256, 128), 1) % 32
    source = (narrow - core) * 16 + jnp.where(lane < 16, core * 16 + lane, (1 - core) * 16 + lane - 16)
    row = lax.broadcasted_iota(jnp.int32, (256, 128), 0)
    pick = jnp.where(row == source, 1.0, 0.0).astype(jnp.bfloat16)
    for i in range(12):
        if i % 3 == 0:
            fetch_a[i // 3].wait()
        block = lax.dot_general(leg_a[i], pick, NN, preferred_element_type=jnp.float32)
        block = block.astype(jnp.bfloat16)
        cols_ref[i, :256] = block
        cols_ref[i, 256:] = block
    fetch_c.wait()
    wide_tiles[...] = tiles[...].astype(jnp.float32)
    half = [wide_tiles[k, pl.ds(pl.multiple_of(core * 8, 8), 8), :] for k in range(12)]
    ops = jnp.concatenate(half, axis=0).astype(jnp.bfloat16)
    ops_ref[...] = ops
    fetch_node.wait()
    leg_c(node_ref, ops, scratch)
    put_first(scratch, first_ref, 0)


def prep(node, leg_ops):
    return pl.pallas_call(
        prep_kernel,
        out_shape=[
            jax.ShapeDtypeStruct((12, 2, 128, 256), jnp.bfloat16),
            jax.ShapeDtypeStruct((12, 512, 128), jnp.bfloat16),
            jax.ShapeDtypeStruct((96, 256), jnp.bfloat16),
        ],
        grid=(1,),
        in_specs=[pl.BlockSpec(memory_space=pltpu.HBM)] * 2,
        out_specs=[pl.BlockSpec(memory_space=pltpu.VMEM)] * 3,
        scratch_shapes=[
            pltpu.VMEM((16, 256, 256), jnp.bfloat16),
            pltpu.VMEM((12, 256, 256), jnp.bfloat16),
            pltpu.VMEM((12, 16, 256), jnp.bfloat16),
            pltpu.VMEM((12, 16, 256), jnp.float32),
            pltpu.VMEM((2, 1536, 128), jnp.float32),
            pltpu.SemaphoreType.DMA((6,)),
        ],
        compiler_params=grant(14),
        cost_estimate=pl.CostEstimate(flops=2 * 3072 * 256 * 300, bytes_accessed=6 << 20, transcendentals=0),
        name="prep",
    )(in_hbm(node), in_hbm(leg_ops))


def sibling_kernel(node_ref, ops_ref, first_ref, out_ref, scratch):
    del first_ref
    leg_c(node_ref, ops_ref[...], scratch)
    put_first(scratch, out_ref, 1)


def add_sibling(node, ops, first):
    return pl.pallas_call(
        sibling_kernel,
        out_shape=jax.ShapeDtypeStruct((12, 2, 128, 256), jnp.bfloat16),
        grid=(1,),
        in_specs=[pl.BlockSpec(memory_space=pltpu.VMEM)] * 3,
        out_specs=pl.BlockSpec(memory_space=pltpu.VMEM),
        scratch_shapes=[pltpu.VMEM((2, 1536, 128), jnp.float32)],
        input_output_aliases={2: 0},
        compiler_params=grant(10),
        cost_estimate=pl.CostEstimate(flops=2 * 1536 * 65536, bytes_accessed=3 << 20, transcendentals=0),
        name="sibling",
    )(node, ops, first)


def table_kernel(index_ref, offset_ref, out_ref):
    shape = (16, 128)
    row, lane = lax.broadcasted_iota(jnp.int32, shape, 0), lax.broadcasted_iota(jnp.int32, shape, 1)
    value = jnp.zeros(shape, jnp.int32)
    for t in range(4):
        for m in range(4):
            entry = offset_ref[t] if m == 3 else index_ref[t, m]
            value = jnp.where(lane == t * 4 + m, entry, value)
    out_ref[...] = jnp.where(row == lax.axis_index("wide"), value, 0)


def own_rows(op_index, offsets):
    smem = pl.BlockSpec(memory_space=pltpu.SMEM)
    return pl.pallas_call(
        table_kernel,
        out_shape=jax.ShapeDtypeStruct((16, 128), jnp.int32),
        in_specs=[smem, smem],
        compiler_params=grant(1),
        name="own_rows",
    )(in_hbm(op_index), in_hbm(offsets))


def main_kernel(table, first_ref, legs_hbm, cols_ref, second, a_own, m1_ref, m2_ref, m3_ref, leg_b, a_abs, a_rel, sem):
    fetch = pltpu.make_async_copy(legs_hbm.at[1], leg_b, sem)
    fetch.start()
    narrow = lax.axis_index("narrow")
    lane = lax.broadcasted_iota(jnp.int32, (16, 128), 1) // 32

    def fill(g, carry):
        starts = []
        for s in range(4):
            start = pl.multiple_of(256 - 32 * table[g, s * 4 + 3], 32)
            starts.append((table[g, s * 4], start))
        for blk in range(16):
            value = None
            for s, (i, start) in enumerate(starts):
                part = cols_ref[i, pl.ds(start + 16 * blk, 16), :]
                value = part if value is None else jnp.where(lane == s, part, value)
            a_abs[g, pl.ds(16 * blk, 16), :] = value
        return carry

    lax.fori_loop(0, 16, fill, 0)
    core, z_lo = lax.rem(narrow, 2), narrow // 8
    y = lax.rem(narrow // 2, 4)
    for blk in range(16):
        dy, dz, dc = blk // 4, (blk // 2) % 2, blk % 2
        block = lax.rem(z_lo + dz, 2) * 8 + lax.rem(y + dy, 4) * 2 + lax.rem(core + dc, 2)
        source = pl.multiple_of(block * 16, 16)
        for g in range(16):
            rows = a_own if blk < 4 else a_rel
            row = 16 * (blk % 4 if blk < 4 else blk - 4)
            rows[row : row + 16, g * 128 : (g + 1) * 128] = a_abs[g, pl.ds(source, 16), :]

    fetch.wait()

    def step(g, carry):
        for s in range(4):
            j, k = table[g, s * 4 + 1], table[g, s * 4 + 2]
            lhs = first_ref[k].reshape(256, 256)
            value = lax.dot_general(lhs, leg_b[j], NT, preferred_element_type=jnp.float32)
            value = value.astype(jnp.bfloat16)
            for half in range(2):
                for q in range(8):
                    where = pl.multiple_of(g * 128 + s * 32 + half * 16, 16)
                    source = half * 128 + q * 16
                    second[q, pl.ds(where, 16), :] = value[source : source + 16]
        return carry

    lax.fori_loop(0, 16, step, 0, unroll=True)
    for q in range(8):
        value = lax.dot_general(a_rel[...], second[q], NN, preferred_element_type=jnp.float32)
        m1_ref[q] = value[:64].astype(jnp.bfloat16)
        m2_ref[q] = value[64:128].astype(jnp.bfloat16)
        m3_ref[q] = value[128:].astype(jnp.bfloat16)


def keep_kernel(second, a_own, keep_ref):
    for q in range(8):
        keep_ref[q] = lax.dot_general(a_own[...], second[q], NN, preferred_element_type=jnp.float32)


def keep_of(second, a_own):
    return pl.pallas_call(
        keep_kernel,
        out_shape=jax.ShapeDtypeStruct((8, 64, 256), jnp.float32),
        in_specs=[pl.BlockSpec(memory_space=pltpu.VMEM)] * 2,
        out_specs=pl.BlockSpec(memory_space=pltpu.VMEM),
        compiler_params=grant(4),
        cost_estimate=pl.CostEstimate(flops=2 * 64 * 2048 * 2048, bytes_accessed=9 << 20, transcendentals=0),
        name="own_target",
    )(second, a_own)


def main_of(table, first, leg_ops, cols):
    return pl.pallas_call(
        main_kernel,
        out_shape=[jax.ShapeDtypeStruct((8, 2048, 256), jnp.bfloat16), jax.ShapeDtypeStruct((64, 2048), jnp.bfloat16)]
        + [jax.ShapeDtypeStruct((8, 64, 256), jnp.bfloat16)] * 3,
        grid_spec=pltpu.PrefetchScalarGridSpec(
            num_scalar_prefetch=1,
            grid=(1,),
            in_specs=[
                pl.BlockSpec(memory_space=pltpu.VMEM),
                pl.BlockSpec(memory_space=pltpu.HBM),
                pl.BlockSpec(memory_space=pltpu.VMEM),
            ],
            out_specs=[pl.BlockSpec(memory_space=pltpu.VMEM)] * 5,
            scratch_shapes=[
                pltpu.VMEM((12, 256, 256), jnp.bfloat16),
                pltpu.VMEM((16, 256, 128), jnp.bfloat16),
                pltpu.VMEM((192, 2048), jnp.bfloat16),
                pltpu.SemaphoreType.DMA(()),
            ],
        ),
        compiler_params=grant(28),
        cost_estimate=pl.CostEstimate(flops=128 * 2 * 256**3, bytes_accessed=8 << 20, transcendentals=0),
        name="two_legs",
    )(table, first, in_hbm(leg_ops), cols)


def y_kernel(keep_ref, r1_ref, r2_ref, r3_ref, keep_out, m01_ref, m10_ref, m11_ref):
    f32 = jnp.float32
    for q in range(8):
        value = keep_ref[q] + r1_ref[q].astype(f32) + r2_ref[q].astype(f32) + r3_ref[q].astype(f32)
        keep_out[q] = value[:16]
        m01_ref[q] = value[16:32].astype(jnp.bfloat16)
        m10_ref[q] = value[32:48].astype(jnp.bfloat16)
        m11_ref[q] = value[48:].astype(jnp.bfloat16)


def y_sum(keep, r1, r2, r3):
    return pl.pallas_call(
        y_kernel,
        out_shape=[jax.ShapeDtypeStruct((8, 16, 256), jnp.float32)]
        + [jax.ShapeDtypeStruct((8, 16, 256), jnp.bfloat16)] * 3,
        compiler_params=grant(6),
        name="sum_y",
    )(keep, r1, r2, r3)


def z_kernel(keep_ref, r01_ref, r10_ref, r11_ref, out_ref, scratch):
    f32 = jnp.float32
    core = lax.rem(lax.axis_index("narrow"), 2)
    for q in range(8):
        mine = keep_ref[q] + r10_ref[q].astype(f32)
        other = r01_ref[q].astype(f32) + r11_ref[q].astype(f32)
        low = jnp.where(core == 0, mine, other)
        high = jnp.where(core == 0, other, mine)
        for c in range(2):
            scratch[c, pl.ds(q, 16, stride=16), :] = low[:, c * 128 : (c + 1) * 128]
            scratch[c, pl.ds(8 + q, 16, stride=16), :] = high[:, c * 128 : (c + 1) * 128]
    for c in range(2):
        out_ref[:, c * 128 : (c + 1) * 128] = scratch[c].astype(jnp.bfloat16)


def z_sum(keep, r01, r10, r11):
    vmem = pl.BlockSpec(memory_space=pltpu.VMEM)
    return pl.pallas_call(
        z_kernel,
        out_shape=jax.ShapeDtypeStruct((256, 256), jnp.bfloat16),
        in_specs=[vmem] * 4,
        out_specs=vmem,
        scratch_shapes=[pltpu.VMEM((2, 256, 128), jnp.float32)],
        compiler_params=grant(3),
        name="sum_z",
    )(keep, r01, r10, r11)


def last_kernel(tau, n0, l0, r0, n1, l1, r1, n2, f0, fl, fr, f2, node_ref, side_ref, out_hbm, sigma, out, sems):
    f32 = jnp.float32
    wide = lax.axis_index("wide")
    z_hi, x = wide // 4, lax.rem(wide, 4)
    row = lax.broadcasted_iota(jnp.int32, (256, 256), 0)
    column = lax.broadcasted_iota(jnp.int32, (256, 256), 1)
    eye = jnp.where(row == column, 1.0, 0.0).astype(jnp.bfloat16)
    pieces = []
    for dx, own, near, (far, slot) in ((0, n0, n1, (n2, 0)), (1, l0, l1, (fl, 1)), (3, r0, r1, (fr, 1))):
        pieces += [(dx, 0, own, 0), (dx, 1, near, 0), (dx, 3, near, 1), (dx, 2, far, slot)]
    pieces += [(2, 0, f0, 0), (2, 1, fl, 0), (2, 3, fr, 0), (2, 2, f2, 0)]
    places = []
    for dx, dz, _, _ in pieces:
        w = lax.rem(z_hi - dz + 4, 4) * 4 + lax.rem(x - dx + 4, 4)
        places.append(pl.ds(pl.multiple_of(w * 16, 16), 16))
    for r in range(16):
        for place, (_, _, ref, slot) in zip(places, pieces):
            sigma[r, place, :] = ref[slot, r * 16 : (r + 1) * 16]
        turned = lax.dot_general(eye, sigma[r], NT, preferred_element_type=f32)
        out[r] = node_ref[r].astype(f32) + tau * (side_ref[r].astype(f32) - turned)
        pltpu.make_async_copy(out.at[r], out_hbm.at[r], sems.at[r]).start()
    for r in range(16):
        pltpu.make_async_copy(out.at[r], out_hbm.at[r], sems.at[r]).wait()


def last_of(tau, pieces, node, side):
    return pl.pallas_call(
        functools.partial(last_kernel, tau),
        out_shape=jax.ShapeDtypeStruct((16, 256, 256), jnp.float32),
        in_specs=[pl.BlockSpec(memory_space=pltpu.VMEM)] * (len(pieces) + 2),
        out_specs=pl.BlockSpec(memory_space=pltpu.HBM),
        scratch_shapes=[
            pltpu.VMEM((16, 256, 256), jnp.bfloat16),
            pltpu.VMEM((16, 256, 256), jnp.float32),
            pltpu.SemaphoreType.DMA((16,)),
        ],
        compiler_params=grant(16),
        name="update",
    )(*pieces, node, side)


def per_device(node, right_side, leg_ops, op_index, offsets):
    tau = 0.5 / math.sqrt(op_index.shape[0] * lax.axis_size("wide"))
    table = own_rows(op_index, offsets)
    for axis in ("x", "z_hi"):
        table = table + sum(send(table, **{f"d{axis}": d}) for d in (1, 3, 2))
    sibling = send(node, dcore=1)
    first, cols, ops_c = prep(node, leg_ops)
    first = add_sibling(sibling, ops_c, first)
    second, a_own, m1, m2, m3 = main_of(table, first, leg_ops, cols)
    r1, r3, r2 = send(m1, dy=1), send(m3, dy=3), send(m2, dy=2)
    keep = keep_of(second, a_own)
    keep, m01, m10, m11 = y_sum(keep, r1, r2, r3)
    r10, r11 = send(m10, dz_lo=1), send(m11, dz_lo=1, dcore=1)
    r01 = send(m01, dcore=1)
    piece = z_sum(keep, r01, r10, r11)
    piece = piece[None]
    z1, z3 = send(piece, dz_hi=1), send(piece, dz_hi=3)
    l0, r0 = send(piece, dx=1), send(piece, dx=3)
    fa = send(z1[:, :128], dz_hi=1)
    near = jnp.concatenate([z1, z3])
    l1, r1 = send(near, dx=1), send(near, dx=3)
    fb = send(z3[:, 128:], dz_hi=3)
    f0 = send(l0, dx=1)
    far = jnp.concatenate([fa, fb], axis=1)
    fl = send(jnp.concatenate([l1[:1], far]), dx=1)
    fr = send(jnp.concatenate([r1[1:], far]), dx=3)
    f2 = send(far, dx=2)
    pieces = (piece, l0, r0, near, l1, r1, far, f0, fl, fr, f2)
    return last_of(tau, pieces, node, right_side)


def solution(mesh):
    in_specs = (P("narrow", None, None), P("narrow", None, None), P(), P("wide", None), P("wide"))
    out_specs = P("narrow", None, None)
    return jax.shard_map(
        per_device, mesh=mesh, in_specs=in_specs, out_specs=out_specs, check_vma=False
    )
```
